512 devices in a mesh: dom: 128 (over z, y, core), src: 4 (over x).
Axes of the slice: x: 4, y: 4, z: 16, core: 2. Of those that a mesh axis runs over, the one named last changes fastest.
Arguments:
- features: bfloat16 [524288, 256], P(('dom', 'src')), may hold values from -6 to 6
- cotangent: bfloat16 [524288, 256], P(('dom', 'src')), may hold values from -6 to 6
- w_self: bfloat16 [256, 256], replicated, may hold values from -0.375 to 0.375
- w_neigh: bfloat16 [256, 256], replicated, may hold values from -0.375 to 0.375
- bias: bfloat16 [256], replicated, may hold values from -3 to 3
- send_rows: int32 [128, 4, 128, 8], P('dom', 'src'), may hold values from -1 to 1023, as said below
- edge_src: int32 [128, 4, 8192], P('dom', 'src'), may hold values from 0 to 2047, as said below
- edge_dst: int32 [128, 4, 8192], P('dom', 'src'), may hold values from 0 to 4095
- tile_count: int32 [128, 4], P('dom', 'src'), may hold values from 16 to 64, as said below
Outputs:
- activations: bfloat16 [524288, 256], P(('dom', 'src'))
- feature_grad: float32 [524288, 256], P(('dom', 'src'))
The draws below stay inside these ranges and needn't reach their ends.
Inputs may be any that keep to these rules, and one draw needn't show every extreme that they name: `send_rows`: slots of a list are filled from the first one; some list of every owner is full; an account's own part sends it nothing. `edge_src`: every edge refers to a local row or to a filled slot. Edge slots after the first tile_count * 128 are ignored.
All inputs are finite; a program needn't handle non-finite values.
Results may differ from the reference program's by a relative error of at most 0.009.
Values may be sent and summed in bfloat16 or wider, within the bound.
No kernel may reach another device: no remote copies, remote signals or barrier semaphores. Data moves between devices by JAX's collectives and lax.ppermute only.
A program may use at most 64 MiB of HBM per device.

```python
import jax
import jax.numpy as jnp
from jax import lax

F = 256
H = 256
TILE = 128
NODE_DEV = 1024
CAP = 8
TILES_DEV = 64
E_DEV = 8192
PART_ROWS = 4096
HALO = 1024
NODES = 524288
N_DOM = 128
N_SRC = 4


def peer_counts(key):
    counts = jax.random.randint(jax.random.fold_in(key, 101), (N_DOM, N_SRC, N_DOM), 1, CAP + 1)
    owner = jnp.arange(N_DOM)[:, None, None]
    reader = jnp.arange(N_DOM)[None, None, :]
    counts = jnp.where(owner == reader, 0, counts)
    counts = jnp.where(reader == (owner + 1) % N_DOM, CAP, counts)
    return counts


def draw_send_rows(key, part):
    counts = peer_counts(key)
    chosen = jax.random.randint(jax.random.fold_in(key, 211), (N_DOM, N_SRC, N_DOM, CAP), 0, NODE_DEV)
    slot_index = jnp.arange(CAP)[None, None, None, :]
    return jnp.where(slot_index < counts[:, :, :, None], chosen, -1).astype(jnp.int32)


def draw_edge_src(key, part):
    counts = peer_counts(key)
    shape = (N_DOM, N_SRC, E_DEV)
    reader = jnp.arange(N_DOM)[:, None, None] + jnp.zeros(shape, jnp.int32)
    column = jnp.arange(N_SRC)[None, :, None] + jnp.zeros(shape, jnp.int32)
    local_pick = jax.random.randint(jax.random.fold_in(key, 307), shape, 0, NODE_DEV)
    offset = jax.random.randint(jax.random.fold_in(key, 311), shape, 0, N_DOM - 1)
    owner = (reader + 1 + offset) % N_DOM
    limit = counts[owner, column, reader]
    slot_pick = jax.random.randint(jax.random.fold_in(key, 313), shape, 0, limit)
    remote_pick = NODE_DEV + owner * CAP + slot_pick
    coin = jax.random.randint(jax.random.fold_in(key, 317), shape, 0, 2)
    result = jnp.where(coin == 0, local_pick, remote_pick)
    result = result.at[0, :, 0].set(NODE_DEV + (N_DOM - 1) * CAP + CAP - 1)
    return result.astype(jnp.int32)


def draw_tile_count(key, part):
    lowest = max(1, TILES_DEV // 4)
    counts = jax.random.randint(jax.random.fold_in(key, 401), (N_DOM * N_SRC,), lowest, TILES_DEV + 1)
    busiest = jax.random.randint(jax.random.fold_in(key, 409), (), 0, N_DOM * N_SRC)
    counts = counts.at[busiest].set(TILES_DEV)
    return counts.reshape(N_DOM, N_SRC).astype(jnp.int32)


def touch_ends(drawn, key, low, top_value):
    longest = drawn.shape.index(max(drawn.shape))
    spots = []
    for shift in (0, 1):
        where = [jax.random.randint(jax.random.fold_in(key, axis), (), 0, length) for axis, length in enumerate(drawn.shape)]
        where[longest] = (where[longest] + shift) % drawn.shape[longest]
        spots.append(tuple(where))
    return drawn.at[spots[0]].set(low).at[spots[1]].set(top_value)


def shard_levels(rng, extent, split, least, largest):
    factor_of = 1.0
    for axis_at, parts in split:
        draws = jax.random.uniform(jax.random.fold_in(jax.random.fold_in(rng, 6), axis_at), (parts,), jnp.float32, least / len(split), largest / len(split))
        factor_of = factor_of * jnp.repeat(jnp.exp(draws), extent[axis_at] // parts).reshape((-1,) + (1,) * (len(extent) - 1 - axis_at))
    return factor_of


def normal_values(stream_key, extent, width, most, shards=(), dtype=jnp.bfloat16):
    entries = jax.random.normal(stream_key, extent, jnp.float32) * width
    if len(shards) > 0:
        entries = shard_levels(stream_key, extent, shards, -0.22, 0.18) * entries
    return jnp.clip(entries, min=-most, max=most).astype(dtype)


def setup_inputs(seed: int = 0) -> dict:
    seeds = jax.random.split(jax.random.key(seed), 10)
    return {
        "features": normal_values(seeds[0], (NODES, F), 1.0, 6.0, ((0, 512),)),
        "cotangent": normal_values(seeds[1], (NODES, H), 1.0, 6.0, ((0, 512),)),
        "w_self": normal_values(seeds[2], (F, H), F ** -0.5, 0.375),
        "w_neigh": normal_values(seeds[3], (F, H), F ** -0.5, 0.375),
        "bias": normal_values(seeds[4], (H,), 0.5, 3.0),
        "send_rows": draw_send_rows(jax.random.fold_in(seeds[9], 71), 0),
        "edge_src": draw_edge_src(jax.random.fold_in(seeds[9], 71), 0),
        "edge_dst": touch_ends(jax.random.randint(seeds[7], (N_DOM, N_SRC, E_DEV), 0, PART_ROWS), jax.random.fold_in(seeds[7], 1), 0, PART_ROWS - 1).astype(jnp.int32),
        "tile_count": draw_tile_count(jax.random.fold_in(seeds[9], 71), 0),
    }


def reference(features, cotangent, w_self, w_neigh, bias, send_rows, edge_src, edge_dst, tile_count):
    blocks = features.reshape(N_DOM, N_SRC, NODE_DEV, F)
    upstreams = cotangent.reshape(N_DOM, N_SRC, NODE_DEV, H)
    peer_index = jnp.arange(N_DOM)
    edge_tile = jnp.arange(E_DEV) // TILE

    def column_data(owner, column):
        senders = send_rows[:, column, owner, :]
        filled = senders >= 0
        active = edge_tile < tile_count[owner, column]
        return senders, filled, active, edge_src[owner, column], edge_dst[owner, column]

    def one_part(returned, owner):
        totals = jnp.zeros((PART_ROWS, F), jnp.float32)
        degree = jnp.zeros((PART_ROWS,), jnp.float32)
        for column in range(N_SRC):
            senders, filled, active, sources, targets = column_data(owner, column)
            fetched = blocks[:, column][peer_index[:, None], jnp.maximum(senders, 0)]
            fetched = jnp.where(filled[:, :, None], fetched, jnp.zeros((), jnp.bfloat16))
            table = jnp.concatenate([blocks[owner, column], fetched.reshape(HALO, F)], axis=0)
            gathered = jnp.where(active[:, None], table[sources], jnp.zeros((), jnp.bfloat16))
            partial_value = jnp.zeros((PART_ROWS, F), jnp.float32).at[targets].add(gathered.astype(jnp.float32))
            rounded = lax.optimization_barrier(partial_value.astype(jnp.bfloat16))
            totals = totals + rounded.astype(jnp.float32)
            degree = degree + jnp.zeros((PART_ROWS,), jnp.float32).at[targets].add(active.astype(jnp.float32))
        inverse = 1.0 / jnp.maximum(degree, 1.0)
        neighbour_mean = (totals * inverse[:, None]).astype(jnp.bfloat16)
        own_rows = blocks[owner].reshape(PART_ROWS, F)
        preact = (jnp.dot(own_rows, w_self, preferred_element_type=jnp.float32)
                  + jnp.dot(neighbour_mean, w_neigh, preferred_element_type=jnp.float32)
                  + bias.astype(jnp.float32))
        sigma = jax.nn.sigmoid(preact)
        outputs = (preact * sigma).astype(jnp.bfloat16)
        slope = sigma * (1.0 + preact * (1.0 - sigma))
        upstream = (upstreams[owner].reshape(PART_ROWS, H).astype(jnp.float32) * slope).astype(jnp.bfloat16)
        grad_own = jnp.dot(upstream, w_self.T, preferred_element_type=jnp.float32)
        scaled = (jnp.dot(upstream, w_neigh.T, preferred_element_type=jnp.float32) * inverse[:, None]).astype(jnp.bfloat16)
        grad_parts = []
        for column in range(N_SRC):
            senders, filled, active, sources, targets = column_data(owner, column)
            contrib = jnp.where(active[:, None], scaled[targets], jnp.zeros((), jnp.bfloat16)).astype(jnp.float32)
            grad_table = jnp.zeros((NODE_DEV + HALO, F), jnp.float32).at[sources].add(contrib)
            grad_parts.append(grad_table[:NODE_DEV])
            remote_grad = grad_table[NODE_DEV:].reshape(N_DOM, CAP, F)
            target_rows = jnp.where(filled, senders, NODE_DEV)
            returned = returned.at[peer_index[:, None], column, target_rows].add(remote_grad, mode="drop")
        grad_feat = grad_own + jnp.concatenate(grad_parts, axis=0)
        return returned, (outputs, grad_feat)

    start = jnp.zeros((N_DOM, N_SRC, NODE_DEV, F), jnp.float32)
    returned, (outputs, grad_feat) = lax.scan(one_part, start, jnp.arange(N_DOM))
    total_grad = grad_feat.reshape(N_DOM, N_SRC, NODE_DEV, F) + returned
    return outputs.reshape(NODES, H), total_grad.reshape(NODES, F)
```

```python
import functools

import jax
import jax.numpy as jnp
from jax import lax
from jax.experimental import pallas as pl
from jax.experimental.pallas import tpu as pltpu
from jax.sharding import PartitionSpec as P

ROWS = 1024
WIDTH = 256
PART = 4096
EDGES = 8192
CHUNK = 512
SUB = 256
WIN = 384
PADDED = PART + WIN
CNT = 16
LOCAL_END = 1 << 22
ACTIVE_END = 1 << 23
F32 = jnp.float32
BF16 = jnp.bfloat16


def one_hot(mask):
    return jnp.where(mask, 1.0, 0.0).astype(BF16)


def iota(shape, dim):
    return lax.broadcasted_iota(jnp.int32, shape, dim)


def key_column(row):
    return jnp.transpose(jnp.broadcast_to(row, (128, 128)))


def source_of(keys, remote):
    return jnp.where((keys >> 22) == remote, keys & 1023, -1)


def target_of(keys):
    return (keys >> 10) & 4095


def local_edges(keys_s):
    def step(i, lo):
        probe = lo + (4096 >> i)
        return jnp.where(keys_s[probe - 1] < LOCAL_END, probe, lo)

    lo = lax.fori_loop(0, 13, step, 0)
    return jnp.where((lo == EDGES - 1) & (keys_s[EDGES - 1] < LOCAL_END), EDGES, lo)


def edge_range(keys_s, active_s, remote):
    boundary = local_edges(keys_s)
    if remote:
        return boundary, active_s[0] * 128
    return 0, boundary


def sub_range(keys_s, start, lo, hi):
    first = jnp.maximum(start, lo)
    last = jnp.minimum(start + SUB - 1, hi - 1)
    base = (target_of(keys_s[first]) // 16) * 16
    count = jnp.where(last >= first, (target_of(keys_s[last]) - base) // WIN + 1, 0)
    return base, count


def aggregate(keys_s, active_s, keys_v, table, acc, remote, ready):
    lo, hi = edge_range(keys_s, active_s, remote)
    ready()

    def tile(t, carry):
        rows = [keys_v[4 * t + j] for j in range(4)]
        parts = []
        for j in range(4):
            src = source_of(key_column(rows[j]), remote)
            parts.append(
                jnp.concatenate(
                    [one_hot(src == iota((128, 128), 1) + 128 * c) for c in range(ROWS // 128)], axis=1
                )
            )
        pick = jnp.concatenate(parts, axis=0)
        got = jnp.dot(pick, table[...], preferred_element_type=F32).astype(BF16)
        for sub in range(CHUNK // SUB):
            base, count = sub_range(keys_s, t * CHUNK + sub * SUB, lo, hi)
            piece = got[sub * SUB : (sub + 1) * SUB]
            targets = [target_of(rows[2 * sub + j]) for j in range(2)]

            def window(w, c):
                off = pl.multiple_of(base + w * WIN, 16)
                place = jnp.concatenate(
                    [one_hot(iota((WIN, 128), 0) + off == targets[j]) for j in range(2)], axis=1
                )
                acc[pl.ds(off, WIN), :] += jnp.dot(place, piece, preferred_element_type=F32)
                return c

            lax.fori_loop(0, count, window, 0)
        return carry

    lax.fori_loop(lo // CHUNK, (hi + CHUNK - 1) // CHUNK, tile, 0)


def forward_local_kernel(keys_s, active_s, keys_v, table, acc, counts):
    acc[...] = jnp.zeros_like(acc)
    aggregate(keys_s, active_s, keys_v, table, acc, 0, lambda: None)

    def tally(t, total):
        keys = [keys_v[4 * t + j] for j in range(4)]
        high = jnp.concatenate(
            [one_hot((iota((32, 128), 0) == (target_of(k) >> 7)) & (k < ACTIVE_END)) for k in keys], axis=1
        )
        low = jnp.concatenate([one_hot(iota((128, 128), 0) == (target_of(k) & 127)) for k in keys], axis=1)
        return total + lax.dot_general(high, low, (((1,), (1,)), ((), ())), preferred_element_type=F32)

    total = lax.fori_loop(0, EDGES // CHUNK, tally, jnp.zeros((32, 128), F32))
    upper = jnp.floor(total * (1.0 / 256.0))
    lower = total - upper * 256.0
    for s in range(4):
        both = jnp.concatenate([upper[8 * s : 8 * s + 8], lower[8 * s : 8 * s + 8]], axis=1)
        counts[s] = jnp.concatenate([both, jnp.zeros((8, WIDTH), F32)], axis=0).astype(BF16)


def forward_remote_kernel(keys_s, active_s, keys_v, table, counts, before, out, acc, sem):
    copy = pltpu.make_async_copy(before, acc, sem)
    copy.start()
    aggregate(keys_s, active_s, keys_v, table, acc, 1, copy.wait)
    for s in range(4):
        out[s, :ROWS, :] = acc[s * ROWS : (s + 1) * ROWS, :].astype(BF16)
        out[s, ROWS:, :] = counts[s]


def dense_kernel(feats, cots, w_self, w_neigh, bias, recv, counts, acts, scaled, own, inv_ref):
    i = pl.program_id(0)

    @pl.when(i == 0)
    def _():
        deg = jnp.zeros((8, 128), F32)
        for s in range(4):
            c = counts[s].astype(F32)
            deg = deg + c[:8, :128] * 256.0 + c[:8, 128:]
        inv = 1.0 / jnp.maximum(deg, 1.0)
        for r in range(8):
            inv_ref[r] = inv[r : r + 1]

    cols = [key_column(inv_ref[2 * i + r]) for r in range(2)]
    inverse = jnp.concatenate([jnp.concatenate([c, c], axis=1) for c in cols], axis=0)
    totals = recv[0].astype(F32)
    for s in range(1, 4):
        totals = totals + recv[s].astype(F32)
    mean = (totals * inverse).astype(BF16)
    pre = (
        jnp.dot(feats[...], w_self[...], preferred_element_type=F32)
        + jnp.dot(mean, w_neigh[...], preferred_element_type=F32)
        + bias[...].astype(F32)
    )
    sigma = jax.nn.sigmoid(pre)
    acts[...] = (pre * sigma).astype(BF16)
    slope = sigma * (1.0 + pre * (1.0 - sigma))
    up = (cots[...].astype(F32) * slope).astype(BF16)
    contract = (((1,), (1,)), ((), ()))
    back = lax.dot_general(up, w_neigh[...], contract, preferred_element_type=F32)
    value = (back * inverse).astype(BF16)
    for s in range(4):
        scaled[s] = value
    own[...] = lax.dot_general(up, w_self[...], contract, preferred_element_type=F32)


def scatter_back(keys_s, active_s, keys_v, spread, rows_ref, acc, remote):
    lo, hi = edge_range(keys_s, active_s, remote)

    def tile(t, carry):
        rows = [keys_v[4 * t + j] for j in range(4)]
        for sub in range(CHUNK // SUB):
            base, count = sub_range(keys_s, t * CHUNK + sub * SUB, lo, hi)
            cols = [target_of(key_column(rows[2 * sub + j])) for j in range(2)]

            def window(w):
                off = pl.multiple_of(base + w * WIN, 16)
                pick = jnp.concatenate(
                    [
                        jnp.concatenate(
                            [one_hot(c - off == iota((128, 128), 1) + 128 * k) for k in range(WIN // 128)], axis=1
                        )
                        for c in cols
                    ],
                    axis=0,
                )
                return jnp.dot(pick, spread[pl.ds(off, WIN), :], preferred_element_type=F32)

            rows_ref[sub * SUB : (sub + 1) * SUB, :] = window(0)

            def more(w, c):
                rows_ref[sub * SUB : (sub + 1) * SUB, :] += window(w)
                return c

            lax.fori_loop(1, count, more, 0)
        place = jnp.concatenate(
            [one_hot(iota((ROWS, 128), 0) == source_of(rows[j], remote)) for j in range(4)], axis=1
        )
        acc[...] += jnp.dot(place, rows_ref[...].astype(BF16), preferred_element_type=F32)
        return carry

    lax.fori_loop(lo // CHUNK, (hi + CHUNK - 1) // CHUNK, tile, 0)


def load_spread(spread_hbm, spread, sem):
    copy = pltpu.make_async_copy(spread_hbm, spread.at[pl.ds(0, PART), :], sem)
    copy.start()
    spread[PART:, :] = jnp.zeros((WIN, WIDTH), BF16)
    copy.wait()


def backward_remote_kernel(keys_s, active_s, keys_v, spread_hbm, out, spread, rows_ref, acc, sem):
    load_spread(spread_hbm, spread, sem)
    acc[...] = jnp.zeros_like(acc)
    scatter_back(keys_s, active_s, keys_v, spread, rows_ref, acc, 1)
    out[...] = acc[...].astype(BF16)


def backward_local_kernel(keys_s, active_s, keys_v, own, spread_hbm, out, spread, rows_ref, sem):
    load_spread(spread_hbm, spread, sem)
    out[...] = own[...]
    scatter_back(keys_s, active_s, keys_v, spread, rows_ref, out, 0)


VMEM = pl.BlockSpec(memory_space=pltpu.VMEM)
ANY = pl.BlockSpec(memory_space=pl.ANY)
PARAMS = pltpu.CompilerParams(vmem_limit_bytes=40 << 20)


def call(kernel, in_specs, out_shape, scratch, name):
    single = not isinstance(out_shape, tuple)
    return pl.pallas_call(
        kernel,
        grid_spec=pltpu.PrefetchScalarGridSpec(
            num_scalar_prefetch=2,
            grid=(),
            in_specs=in_specs,
            out_specs=VMEM if single else tuple(VMEM for _ in out_shape),
            scratch_shapes=scratch,
        ),
        out_shape=out_shape,
        compiler_params=PARAMS,
        name=name,
    )


def local(features, cotangent, w_self, w_neigh, bias, send_rows, edge_src, edge_dst, tile_count):
    peers, capacity = send_rows.shape[2], send_rows.shape[3]
    senders = send_rows.reshape(peers * capacity)
    nodes = jnp.arange(ROWS, dtype=jnp.int32)
    choose = (senders[:, None] == nodes[None, :]).astype(BF16)
    picked = jnp.dot(choose, features, preferred_element_type=F32).astype(BF16)
    remote = lax.all_to_all(
        picked.reshape(peers, capacity, WIDTH), "dom", split_axis=0, concat_axis=0, tiled=True
    ).reshape(peers * capacity, WIDTH)

    sources = edge_src.reshape(EDGES)
    targets = edge_dst.reshape(EDGES)
    active = tile_count.reshape(1)
    live = jnp.arange(EDGES, dtype=jnp.int32) < active[0] * 128
    keys = ((sources >> 10) << 22) + (targets << 10) + (sources & 1023)
    keys_s = lax.sort(jnp.where(live, keys, ACTIVE_END))
    keys_v = keys_s.reshape(EDGES // 128, 1, 128)

    shape = jax.ShapeDtypeStruct
    before, counts = call(
        forward_local_kernel,
        [VMEM, VMEM],
        (shape((PADDED, WIDTH), F32), shape((4, CNT, WIDTH), BF16)),
        [],
        "aggregate_local",
    )(keys_s, active, keys_v, features)
    partial = call(
        forward_remote_kernel,
        [VMEM, VMEM, VMEM, ANY],
        shape((4, ROWS + CNT, WIDTH), BF16),
        [pltpu.VMEM((PADDED, WIDTH), F32), pltpu.SemaphoreType.DMA],
        "aggregate_remote",
    )(keys_s, active, keys_v, remote, counts, before)
    recv = lax.all_to_all(partial, "src", split_axis=0, concat_axis=0, tiled=True)

    block = ROWS // 4
    tile = pl.BlockSpec((block, WIDTH), lambda i: (i, 0))
    whole = pl.BlockSpec((WIDTH, WIDTH), lambda i: (0, 0))
    four = pl.BlockSpec((4, block, WIDTH), lambda i: (0, i, 0))
    acts, scaled, own = pl.pallas_call(
        dense_kernel,
        grid=(4,),
        in_specs=[
            tile,
            tile,
            whole,
            whole,
            pl.BlockSpec((1, WIDTH), lambda i: (0, 0)),
            four,
            pl.BlockSpec((4, CNT, WIDTH), lambda i: (0, ROWS // CNT, 0)),
        ],
        out_specs=(tile, four, tile),
        out_shape=(shape((ROWS, WIDTH), BF16), shape((4, ROWS, WIDTH), BF16), shape((ROWS, WIDTH), F32)),
        scratch_shapes=[pltpu.VMEM((8, 1, 128), F32)],
        compiler_params=PARAMS,
        name="dense_layer",
    )(features, cotangent, w_self, w_neigh, bias.reshape(1, WIDTH), recv, recv)
    spread = lax.all_to_all(scaled, "src", split_axis=0, concat_axis=0, tiled=True).reshape(PART, WIDTH)

    held = [
        pltpu.VMEM((PADDED, WIDTH), BF16),
        pltpu.VMEM((CHUNK, WIDTH), F32),
    ]
    outgoing = call(
        backward_remote_kernel,
        [VMEM, ANY],
        shape((ROWS, WIDTH), BF16),
        held + [pltpu.VMEM((ROWS, WIDTH), F32), pltpu.SemaphoreType.DMA],
        "scatter_remote",
    )(keys_s, active, keys_v, spread)
    returned = lax.all_to_all(
        outgoing.reshape(peers, capacity, WIDTH), "dom", split_axis=0, concat_axis=0, tiled=True
    ).reshape(peers * capacity, WIDTH)
    kept = call(
        backward_local_kernel,
        [VMEM, VMEM, ANY],
        shape((ROWS, WIDTH), F32),
        held + [pltpu.SemaphoreType.DMA],
        "scatter_local",
    )(keys_s, active, keys_v, own, spread)
    place = (nodes[:, None] == senders[None, :]).astype(BF16)
    incoming = jnp.dot(place, returned, preferred_element_type=F32)
    return acts, kept + incoming


def solution(mesh):
    placed = (
        P(("dom", "src"), None),
        P(("dom", "src"), None),
        P(),
        P(),
        P(),
        P("dom", "src", None, None),
        P("dom", "src", None),
        P("dom", "src", None),
        P("dom", "src"),
    )
    return jax.shard_map(
        local,
        mesh=mesh,
        in_specs=placed,
        out_specs=(P(("dom", "src"), None), P(("dom", "src"), None)),
        check_vma=False,
    )
```

```python
import jax
import jax.numpy as jnp
from jax import lax
from jax.experimental import pallas as pl
from jax.experimental.pallas import tpu as pltpu
from jax.sharding import PartitionSpec as P

ROWS = 1024
WIDTH = 256
PART = 4096
EDGES = 8192
CHUNK = 512
UNROLL = 4
SUB = 256
WIN = 384
PADDED = PART + WIN
CNT = 16
LOCAL_END = 1 << 22
ACTIVE_END = 1 << 23
F32 = jnp.float32
BF16 = jnp.bfloat16


def in_hbm(x):
    return pltpu.with_memory_space_constraint(x, pltpu.HBM)


def one_hot(mask):
    return jnp.where(mask, 1.0, 0.0).astype(BF16)


def iota(shape, dim):
    return lax.broadcasted_iota(jnp.int32, shape, dim)


def key_column(row):
    return jnp.transpose(jnp.broadcast_to(row, (128, 128)))


def source_of(keys, remote):
    return jnp.where((keys >> 22) == remote, keys & 1023, -1)


def target_of(keys):
    return (keys >> 10) & 4095


def local_edges(keys_s):
    def step(i, lo):
        probe = lo + (4096 >> i)
        return jnp.where(keys_s[probe - 1] < LOCAL_END, probe, lo)

    lo = lax.fori_loop(0, 13, step, 0)
    return jnp.where((lo == EDGES - 1) & (keys_s[EDGES - 1] < LOCAL_END), EDGES, lo)


def edge_range(keys_s, active_s, remote):
    boundary = local_edges(keys_s)
    if remote:
        return boundary, active_s[0] * 128
    return 0, boundary


def sub_range(keys_s, start, lo, hi):
    first = jnp.maximum(start, lo)
    last = jnp.minimum(start + SUB - 1, hi - 1)
    base = (target_of(keys_s[first]) // 16) * 16
    count = jnp.where(last >= first, (target_of(keys_s[last]) - base) // WIN + 1, 0)
    return base, count


def place_of(targets, off):
    return jnp.concatenate([one_hot(iota((WIN, 128), 0) + off == x) for x in targets], axis=1)


def pick_of(rows, remote):
    parts = []
    for row in rows:
        src = source_of(key_column(row), remote)
        parts.append(
            jnp.concatenate([one_hot(src == iota((128, 128), 1) + 128 * c) for c in range(ROWS // 128)], axis=1)
        )
    return jnp.concatenate(parts, axis=0)


def further_windows(todo, run):
    most = todo[0][1]
    for item in todo[1:]:
        most = jnp.maximum(most, item[1])

    @pl.when(most > 1)
    def _():
        for item in todo:

            def window(w, c):
                run(item, pl.multiple_of(item[0] + w * WIN, 16))
                return c

            lax.fori_loop(1, item[1], window, 0)


def build_adjacency(keys_s, keys_v, adj, lo, hi):
    def tile(t, carry):
        todo = []
        for u in range(UNROLL):
            rows = [keys_v[2 * UNROLL * t + 2 * u + j] for j in range(2)]
            base, count = sub_range(keys_s, (t * UNROLL + u) * SUB, lo, hi)
            base = pl.multiple_of(base, 16)
            targets = [target_of(r) for r in rows]
            first = jnp.dot(place_of(targets, base), pick_of(rows, 1), preferred_element_type=F32).astype(BF16)
            todo.append((base, count, targets, rows, first))
        for base, count, targets, rows, first in todo:
            adj[pl.ds(base, WIN), :] += first

        def run(item, off):
            more = jnp.dot(place_of(item[2], off), pick_of(item[3], 1), preferred_element_type=F32)
            adj[pl.ds(off, WIN), :] += more.astype(BF16)

        further_windows(todo, run)
        return carry

    size = SUB * UNROLL
    lax.fori_loop(lo // size, (hi + size - 1) // size, tile, 0)


def aggregate_local(keys_s, keys_v, table, acc, lo, hi):
    def tile(t, carry):
        rows = [keys_v[2 * UNROLL * t + j] for j in range(2 * UNROLL)]
        got = jnp.dot(pick_of(rows, 0), table[...], preferred_element_type=F32).astype(BF16)
        todo = []
        for u in range(UNROLL):
            base, count = sub_range(keys_s, (t * UNROLL + u) * SUB, lo, hi)
            base = pl.multiple_of(base, 16)
            targets = [target_of(r) for r in rows[2 * u : 2 * u + 2]]
            piece = got[SUB * u : SUB * u + SUB]
            first = jnp.dot(place_of(targets, base), piece, preferred_element_type=F32)
            todo.append((base, count, targets, piece, first))
        for base, count, targets, piece, first in todo:
            acc[pl.ds(base, WIN), :] += first

        def run(item, off):
            acc[pl.ds(off, WIN), :] += jnp.dot(place_of(item[2], off), item[3], preferred_element_type=F32)

        further_windows(todo, run)
        return carry

    size = SUB * UNROLL
    lax.fori_loop(lo // size, (hi + size - 1) // size, tile, 0)


def prepare_kernel(keys_s, active_s, keys_v, table, adj_out, local_out, counts, adj, acc, sems):
    boundary = local_edges(keys_s)
    adj[...] = jnp.zeros_like(adj)
    build_adjacency(keys_s, keys_v, adj, boundary, active_s[0] * 128)
    save_adj = pltpu.make_async_copy(adj.at[pl.ds(0, PART), :], adj_out, sems.at[0])
    save_adj.start()
    acc[...] = jnp.zeros_like(acc)
    aggregate_local(keys_s, keys_v, table, acc, 0, boundary)
    save_acc = pltpu.make_async_copy(acc.at[pl.ds(0, PART), :], local_out, sems.at[1])
    save_acc.start()

    def tally(t, total):
        keys = [keys_v[8 * t + j] for j in range(8)]
        high = jnp.concatenate(
            [one_hot((iota((32, 128), 0) == (target_of(k) >> 7)) & (k < ACTIVE_END)) for k in keys], axis=1
        )
        low = jnp.concatenate([one_hot(iota((128, 128), 0) == (target_of(k) & 127)) for k in keys], axis=1)
        return total + lax.dot_general(high, low, (((1,), (1,)), ((), ())), preferred_element_type=F32)

    total = lax.fori_loop(0, EDGES // 1024, tally, jnp.zeros((32, 128), F32))
    upper = jnp.floor(total * (1.0 / 256.0))
    lower = total - upper * 256.0
    for s in range(4):
        both = jnp.concatenate([upper[8 * s : 8 * s + 8], lower[8 * s : 8 * s + 8]], axis=1)
        counts[s] = jnp.concatenate([both, jnp.zeros((8, WIDTH), F32)], axis=0).astype(BF16)
    save_adj.wait()
    save_acc.wait()


def transpose_kernel(adj, out):
    out[0] = jnp.transpose(adj[...])


def forward_remote_kernel(table, counts, adj_hbm, local_hbm, out_hbm, adj, local_part, out, sems):
    loads = []
    for i in range(PART // CHUNK):
        rows = pl.ds(i * CHUNK, CHUNK)
        loads.append(
            (
                pltpu.make_async_copy(adj_hbm.at[rows, :], adj.at[i], sems.at[0, i]),
                pltpu.make_async_copy(local_hbm.at[rows, :], local_part.at[i], sems.at[1, i]),
            )
        )
        for copy in loads[i]:
            copy.start()
    for s in range(4):
        out[s, ROWS:, :] = counts[s]
    saves = []
    for i in range(PART // CHUNK):
        for copy in loads[i]:
            copy.wait()
        total = local_part[i] + jnp.dot(adj[i], table[...], preferred_element_type=F32)
        s, h = i // 2, i % 2
        out[s, h * CHUNK : h * CHUNK + CHUNK, :] = total.astype(BF16)
        if h == 1:
            saves.append(pltpu.make_async_copy(out.at[s], out_hbm.at[s], sems.at[2, s]))
            saves[s].start()
    for copy in saves:
        copy.wait()


def pick_kernel(senders, table, out, acc):
    for c in range(8):
        col = key_column(senders[c : c + 1, :])
        pick = jnp.concatenate([one_hot(col == iota((128, 128), 1) + 128 * k) for k in range(ROWS // 128)], axis=1)
        acc[:, c, :] = jnp.dot(pick, table[...], preferred_element_type=F32)
    out[...] = acc[...].astype(BF16)


def combine_kernel(senders, returned, kept, out_hbm, out, sems):
    saves = []
    for i in range(4):
        rows = pl.ds(i * (ROWS // 4), ROWS // 4)
        nodes = iota((ROWS // 4, 128), 0) + i * (ROWS // 4)
        place = jnp.concatenate([one_hot(nodes == senders[j]) for j in range(ROWS // 128)], axis=1)
        out[rows, :] = kept[rows, :] + jnp.dot(place, returned[...], preferred_element_type=F32)
        saves.append(pltpu.make_async_copy(out.at[rows, :], out_hbm.at[rows, :], sems.at[i]))
        saves[i].start()
    for copy in saves:
        copy.wait()


def dense_kernel(feats, cots, w_self, w_neigh, bias, recv, counts, acts, scaled, own, inv_ref):
    i = pl.program_id(0)

    @pl.when(i == 0)
    def _():
        deg = jnp.zeros((8, 128), F32)
        for s in range(4):
            c = counts[s].astype(F32)
            deg = deg + c[:8, :128] * 256.0 + c[:8, 128:]
        inv = 1.0 / jnp.maximum(deg, 1.0)
        for r in range(8):
            inv_ref[r] = inv[r : r + 1]

    cols = [key_column(inv_ref[2 * i + r]) for r in range(2)]
    inverse = jnp.concatenate([jnp.concatenate([c, c], axis=1) for c in cols], axis=0)
    totals = recv[0].astype(F32)
    for s in range(1, 4):
        totals = totals + recv[s].astype(F32)
    mean = (totals * inverse).astype(BF16)
    pre = (
        jnp.dot(feats[...], w_self[...], preferred_element_type=F32)
        + jnp.dot(mean, w_neigh[...], preferred_element_type=F32)
        + bias[...].astype(F32)
    )
    sigma = jax.nn.sigmoid(pre)
    acts[...] = (pre * sigma).astype(BF16)
    slope = sigma * (1.0 + pre * (1.0 - sigma))
    up = (cots[...].astype(F32) * slope).astype(BF16)
    contract = (((1,), (1,)), ((), ()))
    back = lax.dot_general(up, w_neigh[...], contract, preferred_element_type=F32)
    value = (back * inverse).astype(BF16)
    for s in range(4):
        scaled[s] = value
    own[...] = lax.dot_general(up, w_self[...], contract, preferred_element_type=F32)


def scatter_back(keys_s, active_s, keys_v, spread, rows_ref, acc, remote):
    lo, hi = edge_range(keys_s, active_s, remote)

    def tile(t, carry):
        rows = [keys_v[4 * t + j] for j in range(4)]
        for sub in range(CHUNK // SUB):
            base, count = sub_range(keys_s, t * CHUNK + sub * SUB, lo, hi)
            cols = [target_of(key_column(rows[2 * sub + j])) for j in range(2)]

            def window(w):
                off = pl.multiple_of(base + w * WIN, 16)
                pick = jnp.concatenate(
                    [
                        jnp.concatenate(
                            [one_hot(c - off == iota((128, 128), 1) + 128 * k) for k in range(WIN // 128)], axis=1
                        )
                        for c in cols
                    ],
                    axis=0,
                )
                return jnp.dot(pick, spread[pl.ds(off, WIN), :], preferred_element_type=F32)

            rows_ref[sub * SUB : (sub + 1) * SUB, :] = window(0)

            def more(w, c):
                rows_ref[sub * SUB : (sub + 1) * SUB, :] += window(w)
                return c

            lax.fori_loop(1, count, more, 0)
        place = jnp.concatenate(
            [one_hot(iota((ROWS, 128), 0) == source_of(rows[j], remote)) for j in range(4)], axis=1
        )
        acc[...] += jnp.dot(place, rows_ref[...].astype(BF16), preferred_element_type=F32)
        return carry

    lax.fori_loop(lo // CHUNK, (hi + CHUNK - 1) // CHUNK, tile, 0)


def load_spread(spread_hbm, spread, sem):
    copy = pltpu.make_async_copy(spread_hbm, spread.at[pl.ds(0, PART), :], sem)
    copy.start()
    spread[PART:, :] = jnp.zeros((WIN, WIDTH), BF16)
    copy.wait()


def backward_remote_kernel(spread, adj_hbm, out, adj, sems):
    loads = [pltpu.make_async_copy(adj_hbm.at[i], adj.at[i], sems.at[i]) for i in range(PART // CHUNK)]
    for copy in loads:
        copy.start()
    total = jnp.zeros((ROWS, WIDTH), F32)
    for i, copy in enumerate(loads):
        copy.wait()
        total = total + jnp.dot(adj[i], spread[i * CHUNK : i * CHUNK + CHUNK, :], preferred_element_type=F32)
    out[...] = total.astype(BF16)


def backward_local_kernel(keys_s, active_s, keys_v, own, spread_hbm, out, spread, rows_ref, sem):
    load_spread(spread_hbm, spread, sem)
    out[...] = own[...]
    scatter_back(keys_s, active_s, keys_v, spread, rows_ref, out, 0)


VMEM = pl.BlockSpec(memory_space=pltpu.VMEM)
ANY = pl.BlockSpec(memory_space=pl.ANY)
HBM = pl.BlockSpec(memory_space=pltpu.HBM)
PARAMS = pltpu.CompilerParams(vmem_limit_bytes=30 << 20)


def call(kernel, in_specs, out_shape, scratch, name):
    single = not isinstance(out_shape, tuple)
    return pl.pallas_call(
        kernel,
        grid_spec=pltpu.PrefetchScalarGridSpec(
            num_scalar_prefetch=2,
            grid=(),
            in_specs=in_specs,
            out_specs=VMEM if single else tuple(VMEM for _ in out_shape),
            scratch_shapes=scratch,
        ),
        out_shape=out_shape,
        compiler_params=PARAMS,
        name=name,
    )


def local(features, cotangent, w_self, w_neigh, bias, send_rows, edge_src, edge_dst, tile_count):
    peers, capacity = send_rows.shape[2], send_rows.shape[3]
    shape = jax.ShapeDtypeStruct
    picked = pl.pallas_call(
        pick_kernel,
        grid=(1,),
        in_specs=[
            pl.BlockSpec((capacity, peers), lambda i: (0, 0)),
            pl.BlockSpec((ROWS, WIDTH), lambda i: (0, 0)),
        ],
        out_specs=pl.BlockSpec((peers, capacity, WIDTH), lambda i: (0, 0, 0)),
        out_shape=shape((peers, capacity, WIDTH), BF16),
        scratch_shapes=[pltpu.VMEM((peers, capacity, WIDTH), F32)],
        compiler_params=PARAMS,
        name="pick_rows",
    )(in_hbm(jnp.transpose(send_rows.reshape(peers, capacity))), in_hbm(features))
    remote = lax.all_to_all(picked, "dom", split_axis=0, concat_axis=0, tiled=True).reshape(peers * capacity, WIDTH)

    sources = edge_src.reshape(EDGES)
    targets = edge_dst.reshape(EDGES)
    active = tile_count.reshape(1)
    live = jnp.arange(EDGES, dtype=jnp.int32) < active[0] * 128
    keys = ((sources >> 10) << 22) + (targets << 10) + (sources & 1023)
    keys_s = lax.sort(jnp.where(live, keys, ACTIVE_END))
    keys_v = keys_s.reshape(EDGES // 128, 1, 128)

    adj, before, counts = pl.pallas_call(
        prepare_kernel,
        grid_spec=pltpu.PrefetchScalarGridSpec(
            num_scalar_prefetch=2,
            grid=(),
            in_specs=[VMEM, VMEM],
            out_specs=(HBM, HBM, VMEM),
            scratch_shapes=[
                pltpu.VMEM((PADDED, ROWS), BF16),
                pltpu.VMEM((PADDED, WIDTH), F32),
                pltpu.SemaphoreType.DMA((2,)),
            ],
        ),
        out_shape=(
            pltpu.HBM((PART, ROWS), BF16),
            pltpu.HBM((PART, WIDTH), F32),
            shape((4, CNT, WIDTH), BF16),
        ),
        compiler_params=PARAMS,
        name="prepare",
    )(keys_s, active, keys_v, features)
    chunks = PART // CHUNK
    partial = pl.pallas_call(
        forward_remote_kernel,
        in_specs=[VMEM, VMEM, HBM, HBM],
        out_specs=HBM,
        out_shape=pltpu.HBM((4, ROWS + CNT, WIDTH), BF16),
        scratch_shapes=[
            pltpu.VMEM((chunks, CHUNK, ROWS), BF16),
            pltpu.VMEM((chunks, CHUNK, WIDTH), F32),
            pltpu.VMEM((4, ROWS + CNT, WIDTH), BF16),
            pltpu.SemaphoreType.DMA((3, chunks)),
        ],
        compiler_params=PARAMS,
        name="aggregate_remote",
    )(remote, counts, in_hbm(adj), in_hbm(before))
    recv = lax.all_to_all(partial, "src", split_axis=0, concat_axis=0, tiled=True)
    adj, partial = lax.optimization_barrier((adj, partial))
    adj_t = pl.pallas_call(
        transpose_kernel,
        grid=(chunks,),
        in_specs=[pl.BlockSpec((CHUNK, ROWS), lambda i: (i, 0))],
        out_specs=pl.BlockSpec((1, ROWS, CHUNK), lambda i: (i, 0, 0)),
        out_shape=pltpu.HBM((chunks, ROWS, CHUNK), BF16),
        compiler_params=PARAMS,
        name="adjacency_transposed",
    )(in_hbm(adj))

    block = ROWS // 4
    tile = pl.BlockSpec((block, WIDTH), lambda i: (i, 0))
    whole = pl.BlockSpec((WIDTH, WIDTH), lambda i: (0, 0))
    four = pl.BlockSpec((4, block, WIDTH), lambda i: (0, i, 0))
    acts, scaled, own = pl.pallas_call(
        dense_kernel,
        grid=(4,),
        in_specs=[
            tile,
            tile,
            whole,
            whole,
            pl.BlockSpec((1, WIDTH), lambda i: (0, 0)),
            four,
            pl.BlockSpec((4, CNT, WIDTH), lambda i: (0, ROWS // CNT, 0)),
        ],
        out_specs=(tile, four, tile),
        out_shape=(shape((ROWS, WIDTH), BF16), pltpu.HBM((4, ROWS, WIDTH), BF16), pltpu.HBM((ROWS, WIDTH), F32)),
        scratch_shapes=[pltpu.VMEM((8, 1, 128), F32)],
        compiler_params=PARAMS,
        name="dense_layer",
    )(features, in_hbm(cotangent), w_self, w_neigh, bias.reshape(1, WIDTH), recv, recv)
    spread = lax.all_to_all(scaled, "src", split_axis=0, concat_axis=0, tiled=True).reshape(PART, WIDTH)

    held = [
        pltpu.VMEM((PADDED, WIDTH), BF16),
        pltpu.VMEM((CHUNK, WIDTH), F32),
    ]
    outgoing = pl.pallas_call(
        backward_remote_kernel,
        in_specs=[VMEM, HBM],
        out_specs=VMEM,
        out_shape=pltpu.HBM((ROWS, WIDTH), BF16),
        scratch_shapes=[pltpu.VMEM((chunks, ROWS, CHUNK), BF16), pltpu.SemaphoreType.DMA((chunks,))],
        compiler_params=PARAMS,
        name="scatter_remote",
    )(spread, in_hbm(adj_t))
    returned = lax.all_to_all(
        outgoing.reshape(peers, capacity, WIDTH), "dom", split_axis=0, concat_axis=0, tiled=True
    ).reshape(peers * capacity, WIDTH)
    kept = call(
        backward_local_kernel,
        [VMEM, VMEM, ANY],
        shape((ROWS, WIDTH), F32),
        held + [pltpu.SemaphoreType.DMA],
        "scatter_local",
    )(keys_s, active, keys_v, own, spread)
    total = pl.pallas_call(
        combine_kernel,
        in_specs=[VMEM] * 3,
        out_specs=HBM,
        out_shape=pltpu.HBM((ROWS, WIDTH), F32),
        scratch_shapes=[pltpu.VMEM((ROWS, WIDTH), F32), pltpu.SemaphoreType.DMA((4,))],
        compiler_params=PARAMS,
        name="combine",
    )(send_rows.reshape(peers * capacity // 128, 1, 128), returned, kept)
    return acts, total


def solution(mesh):
    placed = (
        P(("dom", "src"), None),
        P(("dom", "src"), None),
        P(),
        P(),
        P(),
        P("dom", "src", None, None),
        P("dom", "src", None),
        P("dom", "src", None),
        P("dom", "src"),
    )
    return jax.shard_map(
        local,
        mesh=mesh,
        in_specs=placed,
        out_specs=(P(("dom", "src"), None), P(("dom", "src"), None)),
        check_vma=False,
    )
```

```python
import functools

import jax
import jax.numpy as jnp
from jax import lax
from jax.experimental import pallas as pl
from jax.experimental.pallas import tpu as pltpu
from jax.sharding import PartitionSpec as P

ROWS = 1024
WIDTH = 256
PART = 4096
EDGES = 8192
CHUNK = 512
UNROLL = 4
SUB = 256
WIN = 384
PADDED = PART + WIN
CNT = 16
LOCAL_END = 1 << 22
ACTIVE_END = 1 << 23
F32 = jnp.float32
BF16 = jnp.bfloat16


def in_hbm(x):
    return pltpu.with_memory_space_constraint(x, pltpu.HBM)


def one_hot(mask):
    return jnp.where(mask, 1.0, 0.0).astype(BF16)


def iota(shape, dim):
    return lax.broadcasted_iota(jnp.int32, shape, dim)


def key_column(row):
    return jnp.transpose(jnp.broadcast_to(row, (128, 128)))


def source_of(keys, remote):
    return jnp.where((keys >> 22) == remote, keys & 1023, -1)


def target_of(keys):
    return (keys >> 10) & 4095


def local_edges(keys_s):
    def step(i, lo):
        probe = lo + (4096 >> i)
        return jnp.where(keys_s[probe - 1] < LOCAL_END, probe, lo)

    lo = lax.fori_loop(0, 13, step, 0)
    return jnp.where((lo == EDGES - 1) & (keys_s[EDGES - 1] < LOCAL_END), EDGES, lo)


def edge_range(keys_s, active_s, remote):
    boundary = local_edges(keys_s)
    if remote:
        return boundary, active_s[0] * 128
    return 0, boundary


def sub_range(keys_s, start, lo, hi):
    first = jnp.maximum(start, lo)
    last = jnp.minimum(start + SUB - 1, hi - 1)
    base = (target_of(keys_s[first]) // 16) * 16
    count = jnp.where(last >= first, (target_of(keys_s[last]) - base) // WIN + 1, 0)
    return base, count


def place_of(targets, off):
    return jnp.concatenate([one_hot(iota((WIN, 128), 0) + off == x) for x in targets], axis=1)


def pick_of(rows, remote):
    parts = []
    for row in rows:
        src = source_of(key_column(row), remote)
        parts.append(
            jnp.concatenate([one_hot(src == iota((128, 128), 1) + 128 * c) for c in range(ROWS // 128)], axis=1)
        )
    return jnp.concatenate(parts, axis=0)


def further_windows(todo, run):
    most = todo[0][1]
    for item in todo[1:]:
        most = jnp.maximum(most, item[1])

    @pl.when(most > 1)
    def _():
        for item in todo:

            def window(w, c):
                run(item, pl.multiple_of(item[0] + w * WIN, 16))
                return c

            lax.fori_loop(1, item[1], window, 0)


def build_adjacency(keys_s, keys_v, adj, lo, hi):
    def tile(t, carry):
        todo = []
        for u in range(UNROLL):
            rows = [keys_v[2 * UNROLL * t + 2 * u + j] for j in range(2)]
            base, count = sub_range(keys_s, (t * UNROLL + u) * SUB, lo, hi)
            base = pl.multiple_of(base, 16)
            targets = [target_of(r) for r in rows]
            first = jnp.dot(place_of(targets, base), pick_of(rows, 1), preferred_element_type=F32).astype(BF16)
            todo.append((base, count, targets, rows, first))
        for base, count, targets, rows, first in todo:
            adj[pl.ds(base, WIN), :] += first

        def run(item, off):
            more = jnp.dot(place_of(item[2], off), pick_of(item[3], 1), preferred_element_type=F32)
            adj[pl.ds(off, WIN), :] += more.astype(BF16)

        further_windows(todo, run)
        return carry

    size = SUB * UNROLL
    lax.fori_loop(lo // size, (hi + size - 1) // size, tile, 0)


def aggregate_local(keys_s, keys_v, table, acc, lo, hi):
    def tile(t, carry):
        rows = [keys_v[2 * UNROLL * t + j] for j in range(2 * UNROLL)]
        got = jnp.dot(pick_of(rows, 0), table[...], preferred_element_type=F32).astype(BF16)
        todo = []
        for u in range(UNROLL):
            base, count = sub_range(keys_s, (t * UNROLL + u) * SUB, lo, hi)
            base = pl.multiple_of(base, 16)
            targets = [target_of(r) for r in rows[2 * u : 2 * u + 2]]
            piece = got[SUB * u : SUB * u + SUB]
            first = jnp.dot(place_of(targets, base), piece, preferred_element_type=F32)
            todo.append((base, count, targets, piece, first))
        for base, count, targets, piece, first in todo:
            acc[pl.ds(base, WIN), :] += first

        def run(item, off):
            acc[pl.ds(off, WIN), :] += jnp.dot(place_of(item[2], off), item[3], preferred_element_type=F32)

        further_windows(todo, run)
        return carry

    size = SUB * UNROLL
    lax.fori_loop(lo // size, (hi + size - 1) // size, tile, 0)


def prepare_kernel(keys_s, active_s, keys_v, table, adj_out, local_out, counts, adj, acc, sems):
    boundary = local_edges(keys_s)
    adj[...] = jnp.zeros_like(adj)
    build_adjacency(keys_s, keys_v, adj, boundary, active_s[0] * 128)
    save_adj = pltpu.make_async_copy(adj.at[pl.ds(0, PART), :], adj_out, sems.at[0])
    save_adj.start()
    acc[...] = jnp.zeros_like(acc)
    aggregate_local(keys_s, keys_v, table, acc, 0, boundary)
    save_acc = pltpu.make_async_copy(acc.at[pl.ds(0, PART), :], local_out, sems.at[1])
    save_acc.start()

    def tally(t, total):
        keys = [keys_v[8 * t + j] for j in range(8)]
        high = jnp.concatenate(
            [one_hot((iota((32, 128), 0) == (target_of(k) >> 7)) & (k < ACTIVE_END)) for k in keys], axis=1
        )
        low = jnp.concatenate([one_hot(iota((128, 128), 0) == (target_of(k) & 127)) for k in keys], axis=1)
        return total + lax.dot_general(high, low, (((1,), (1,)), ((), ())), preferred_element_type=F32)

    total = lax.fori_loop(0, EDGES // 1024, tally, jnp.zeros((32, 128), F32))
    upper = jnp.floor(total * (1.0 / 256.0))
    lower = total - upper * 256.0
    for s in range(4):
        both = jnp.concatenate([upper[8 * s : 8 * s + 8], lower[8 * s : 8 * s + 8]], axis=1)
        counts[s] = jnp.concatenate([both, jnp.zeros((8, WIDTH), F32)], axis=0).astype(BF16)
    save_adj.wait()
    save_acc.wait()


def transpose_kernel(adj, out):
    out[0] = jnp.transpose(adj[...])


def forward_remote_kernel(shifts, owner_s, table, counts, adj_hbm, local_hbm, *refs):
    outs, (adj, local_part, sems) = refs[:-3], refs[-3:]
    halves = ROWS // CHUNK
    loads = []
    for n in range(len(outs)):
        for h in range(halves):
            rows = pl.ds(pl.multiple_of(owner_s[shifts[n]] * ROWS + h * CHUNK, CHUNK), CHUNK)
            i = n * halves + h
            pair = (
                pltpu.make_async_copy(adj_hbm.at[rows, :], adj.at[i], sems.at[0, i]),
                pltpu.make_async_copy(local_hbm.at[rows, :], local_part.at[i], sems.at[1, i]),
            )
            for copy in pair:
                copy.start()
            loads.append(pair)
    for n, out in enumerate(outs):
        out[ROWS:, :] = counts[owner_s[shifts[n]]]
        for h in range(halves):
            i = n * halves + h
            for copy in loads[i]:
                copy.wait()
            total = local_part[i] + jnp.dot(adj[i], table[...], preferred_element_type=F32)
            out[h * CHUNK : h * CHUNK + CHUNK, :] = total.astype(BF16)


def pick_kernel(senders, table, out, acc):
    for c in range(8):
        col = key_column(senders[c : c + 1, :])
        pick = jnp.concatenate([one_hot(col == iota((128, 128), 1) + 128 * k) for k in range(ROWS // 128)], axis=1)
        acc[:, c, :] = jnp.dot(pick, table[...], preferred_element_type=F32)
    out[...] = acc[...].astype(BF16)


def combine_kernel(senders, returned, kept, out_hbm, out, sems):
    saves = []
    for i in range(4):
        rows = pl.ds(i * (ROWS // 4), ROWS // 4)
        nodes = iota((ROWS // 4, 128), 0) + i * (ROWS // 4)
        place = jnp.concatenate([one_hot(nodes == senders[j]) for j in range(ROWS // 128)], axis=1)
        out[rows, :] = kept[rows, :] + jnp.dot(place, returned[...], preferred_element_type=F32)
        saves.append(pltpu.make_async_copy(out.at[rows, :], out_hbm.at[rows, :], sems.at[i]))
        saves[i].start()
    for copy in saves:
        copy.wait()


def dense_kernel(feats, cots, w_self, w_neigh, bias, *refs):
    parts, counts, (acts, scaled, up_out, inv_ref) = refs[:4], refs[4:8], refs[8:]
    i = pl.program_id(0)

    @pl.when(i == 0)
    def _():
        deg = jnp.zeros((8, 128), F32)
        for s in range(4):
            c = counts[s][...].astype(F32)
            deg = deg + c[:8, :128] * 256.0 + c[:8, 128:]
        inv = 1.0 / jnp.maximum(deg, 1.0)
        for r in range(8):
            inv_ref[r] = inv[r : r + 1]

    cols = [key_column(inv_ref[2 * i + r]) for r in range(2)]
    inverse = jnp.concatenate([jnp.concatenate([c, c], axis=1) for c in cols], axis=0)
    totals = parts[0][...].astype(F32)
    for s in range(1, 4):
        totals = totals + parts[s][...].astype(F32)
    mean = (totals * inverse).astype(BF16)
    pre = (
        jnp.dot(feats[...], w_self[...], preferred_element_type=F32)
        + jnp.dot(mean, w_neigh[...], preferred_element_type=F32)
        + bias[...].astype(F32)
    )
    sigma = jax.nn.sigmoid(pre)
    acts[...] = (pre * sigma).astype(BF16)
    slope = sigma * (1.0 + pre * (1.0 - sigma))
    up = (cots[...].astype(F32) * slope).astype(BF16)
    back = lax.dot_general(up, w_neigh[...], (((1,), (1,)), ((), ())), preferred_element_type=F32)
    scaled[...] = (back * inverse).astype(BF16)
    up_out[...] = up


def scatter_back(keys_s, active_s, keys_v, spread, rows_ref, acc, remote):
    lo, hi = edge_range(keys_s, active_s, remote)

    def tile(t, carry):
        rows = [keys_v[4 * t + j] for j in range(4)]
        for sub in range(CHUNK // SUB):
            base, count = sub_range(keys_s, t * CHUNK + sub * SUB, lo, hi)
            cols = [target_of(key_column(rows[2 * sub + j])) for j in range(2)]

            def window(w):
                off = pl.multiple_of(base + w * WIN, 16)
                pick = jnp.concatenate(
                    [
                        jnp.concatenate(
                            [one_hot(c - off == iota((128, 128), 1) + 128 * k) for k in range(WIN // 128)], axis=1
                        )
                        for c in cols
                    ],
                    axis=0,
                )
                return jnp.dot(pick, spread[pl.ds(off, WIN), :], preferred_element_type=F32)

            rows_ref[sub * SUB : (sub + 1) * SUB, :] = window(0)

            def more(w, c):
                rows_ref[sub * SUB : (sub + 1) * SUB, :] += window(w)
                return c

            lax.fori_loop(1, count, more, 0)
        place = jnp.concatenate(
            [one_hot(iota((ROWS, 128), 0) == source_of(rows[j], remote)) for j in range(4)], axis=1
        )
        acc[...] += jnp.dot(place, rows_ref[...].astype(BF16), preferred_element_type=F32)
        return carry

    lax.fori_loop(lo // CHUNK, (hi + CHUNK - 1) // CHUNK, tile, 0)


def piece_sum(owner_s, pieces, adj, start):
    halves = ROWS // CHUNK
    total = start
    for shift, piece in pieces:
        for h in range(halves):
            rows = piece[h * CHUNK : h * CHUNK + CHUNK, :]
            part = jnp.dot(adj[owner_s[shift] * halves + h], rows, preferred_element_type=F32)
            total = part if total is None else total + part
    return total


def backward_near_kernel(owner_s, own, left, right, adj, out):
    out[...] = piece_sum(owner_s, ((0, own), (3, left), (1, right)), adj, None)


def backward_far_kernel(owner_s, far, near, adj, out):
    out[...] = piece_sum(owner_s, ((2, far),), adj, near[...]).astype(BF16)


def backward_local_kernel(keys_s, active_s, owner_s, keys_v, up, w_self, p0, p1, p2, p3, out, spread, rows_ref, sems):
    loads = []
    for n, (shift, piece) in enumerate(((0, p0), (3, p1), (1, p2), (2, p3))):
        rows = pl.ds(pl.multiple_of(owner_s[shift] * ROWS, ROWS), ROWS)
        loads.append(pltpu.make_async_copy(piece, spread.at[rows, :], sems.at[n]))
        loads[n].start()
    spread[PART:, :] = jnp.zeros((WIN, WIDTH), BF16)
    out[...] = lax.dot_general(up[...], w_self[...], (((1,), (1,)), ((), ())), preferred_element_type=F32)
    for copy in loads:
        copy.wait()
    scatter_back(keys_s, active_s, keys_v, spread, rows_ref, out, 0)


VMEM = pl.BlockSpec(memory_space=pltpu.VMEM)
ANY = pl.BlockSpec(memory_space=pl.ANY)
HBM = pl.BlockSpec(memory_space=pltpu.HBM)
def params(mib):
    return pltpu.CompilerParams(vmem_limit_bytes=mib << 20)


def local(features, cotangent, w_self, w_neigh, bias, send_rows, edge_src, edge_dst, tile_count):
    peers, capacity = send_rows.shape[2], send_rows.shape[3]
    shape = jax.ShapeDtypeStruct
    picked = pl.pallas_call(
        pick_kernel,
        grid=(1,),
        in_specs=[
            pl.BlockSpec((capacity, peers), lambda i: (0, 0)),
            pl.BlockSpec((ROWS, WIDTH), lambda i: (0, 0)),
        ],
        out_specs=pl.BlockSpec((peers, capacity, WIDTH), lambda i: (0, 0, 0)),
        out_shape=shape((peers, capacity, WIDTH), BF16),
        scratch_shapes=[pltpu.VMEM((peers, capacity, WIDTH), F32)],
        compiler_params=params(8),
        name="pick_rows",
    )(in_hbm(jnp.transpose(send_rows.reshape(peers, capacity))), in_hbm(features))
    remote = lax.all_to_all(picked, "dom", split_axis=0, concat_axis=0, tiled=True).reshape(peers * capacity, WIDTH)

    sources = edge_src.reshape(EDGES)
    targets = edge_dst.reshape(EDGES)
    active = tile_count.reshape(1)
    live = jnp.arange(EDGES, dtype=jnp.int32) < active[0] * 128
    keys = ((sources >> 10) << 22) + (targets << 10) + (sources & 1023)
    keys_s = lax.sort(jnp.where(live, keys, ACTIVE_END))
    keys_v = keys_s.reshape(EDGES // 128, 1, 128)

    adj, before, counts = pl.pallas_call(
        prepare_kernel,
        grid_spec=pltpu.PrefetchScalarGridSpec(
            num_scalar_prefetch=2,
            grid=(),
            in_specs=[VMEM, VMEM],
            out_specs=(HBM, HBM, VMEM),
            scratch_shapes=[
                pltpu.VMEM((PADDED, ROWS), BF16),
                pltpu.VMEM((PADDED, WIDTH), F32),
                pltpu.SemaphoreType.DMA((2,)),
            ],
        ),
        out_shape=(
            pltpu.HBM((PART, ROWS), BF16),
            pltpu.HBM((PART, WIDTH), F32),
            shape((4, CNT, WIDTH), BF16),
        ),
        compiler_params=params(30),
        name="prepare",
    )(keys_s, active, keys_v, features)
    chunks = PART // CHUNK
    rank = lax.axis_index("src")

    order = lax.optimization_barrier((rank + jnp.arange(4, dtype=jnp.int32)) % 4)

    def shifted(x, k):
        return lax.ppermute(x, "src", [(j, (j + k) % 4) for j in range(4)])

    def partials(table, *shifts):
        count = len(shifts)
        return pl.pallas_call(
            functools.partial(forward_remote_kernel, shifts),
            grid_spec=pltpu.PrefetchScalarGridSpec(
                num_scalar_prefetch=1,
                grid=(),
                in_specs=[VMEM, VMEM, HBM, HBM],
                out_specs=[VMEM] * count,
                scratch_shapes=[
                    pltpu.VMEM((2 * count, CHUNK, ROWS), BF16),
                    pltpu.VMEM((2 * count, CHUNK, WIDTH), F32),
                    pltpu.SemaphoreType.DMA((2, 2 * count)),
                ],
            ),
            out_shape=[shape((ROWS + CNT, WIDTH), BF16)] * count,
            compiler_params=params(12),
            name="aggregate_remote_" + "_".join(str(k) for k in shifts),
        )(order, table, counts, in_hbm(adj), in_hbm(before))

    (partial_far,) = partials(remote, 2)
    from_far = shifted(partial_far, 2)
    remote, partial_far = lax.optimization_barrier((remote, partial_far))
    partial_next, partial_prev = partials(remote, 1, 3)
    from_prev = shifted(partial_next, 1)
    from_next = shifted(partial_prev, 3)
    remote, partial = lax.optimization_barrier((remote, partial_next))
    (partial_own,) = partials(remote, 0)
    adj, partial = lax.optimization_barrier((adj, partial))
    adj_t = pl.pallas_call(
        transpose_kernel,
        grid=(chunks,),
        in_specs=[pl.BlockSpec((CHUNK, ROWS), lambda i: (i, 0))],
        out_specs=pl.BlockSpec((1, ROWS, CHUNK), lambda i: (i, 0, 0)),
        out_shape=shape((chunks, ROWS, CHUNK), BF16),
        compiler_params=params(10),
        name="adjacency_transposed",
    )(in_hbm(adj))
    adj_t, from_far = lax.optimization_barrier((adj_t, from_far))

    block = ROWS // 4
    tile = pl.BlockSpec((block, WIDTH), lambda i: (i, 0))
    whole = pl.BlockSpec((WIDTH, WIDTH), lambda i: (0, 0))
    count_rows = pl.BlockSpec((CNT, WIDTH), lambda i: (ROWS // CNT, 0))
    received = (partial_own, from_prev, from_next, from_far)
    acts, scaled, up = pl.pallas_call(
        dense_kernel,
        grid=(4,),
        in_specs=[tile, tile, whole, whole, pl.BlockSpec((1, WIDTH), lambda i: (0, 0))]
        + [tile] * 4
        + [count_rows] * 4,
        out_specs=(tile, tile, tile),
        out_shape=(shape((ROWS, WIDTH), BF16), pltpu.HBM((ROWS, WIDTH), BF16), pltpu.HBM((ROWS, WIDTH), BF16)),
        scratch_shapes=[pltpu.VMEM((8, 1, 128), F32)],
        compiler_params=params(10),
        name="dense_layer",
    )(features, in_hbm(cotangent), w_self, w_neigh, bias.reshape(1, WIDTH), *received, *received)
    far = shifted(scaled, 2)
    prev = shifted(scaled, 1)
    follow = shifted(scaled, 3)

    def backward(kernel, pieces, dtype, name):
        return pl.pallas_call(
            kernel,
            grid_spec=pltpu.PrefetchScalarGridSpec(
                num_scalar_prefetch=1, grid=(), in_specs=[VMEM] * (len(pieces) + 1), out_specs=VMEM
            ),
            out_shape=shape((ROWS, WIDTH), dtype),
            compiler_params=params(8),
            name=name,
        )(order, *pieces, adj_t)

    near = backward(backward_near_kernel, (scaled, prev, follow), F32, "scatter_near")
    outgoing = backward(backward_far_kernel, (far, near), BF16, "scatter_far")
    returned = lax.all_to_all(
        outgoing.reshape(peers, capacity, WIDTH), "dom", split_axis=0, concat_axis=0, tiled=True
    ).reshape(peers * capacity, WIDTH)
    kept = pl.pallas_call(
        backward_local_kernel,
        grid_spec=pltpu.PrefetchScalarGridSpec(
            num_scalar_prefetch=3,
            grid=(),
            in_specs=[VMEM] * 3 + [ANY] * 4,
            out_specs=VMEM,
            scratch_shapes=[
                pltpu.VMEM((PADDED, WIDTH), BF16),
                pltpu.VMEM((CHUNK, WIDTH), F32),
                pltpu.SemaphoreType.DMA((4,)),
            ],
        ),
        out_shape=shape((ROWS, WIDTH), F32),
        compiler_params=params(10),
        name="scatter_local",
    )(keys_s, active, order, keys_v, up, w_self, scaled, prev, follow, far)
    total = pl.pallas_call(
        combine_kernel,
        in_specs=[VMEM] * 3,
        out_specs=HBM,
        out_shape=pltpu.HBM((ROWS, WIDTH), F32),
        scratch_shapes=[pltpu.VMEM((ROWS, WIDTH), F32), pltpu.SemaphoreType.DMA((4,))],
        compiler_params=params(8),
        name="combine",
    )(send_rows.reshape(peers * capacity // 128, 1, 128), returned, kept)
    return acts, total


def solution(mesh):
    placed = (
        P(("dom", "src"), None),
        P(("dom", "src"), None),
        P(),
        P(),
        P(),
        P("dom", "src", None, None),
        P("dom", "src", None),
        P("dom", "src", None),
        P("dom", "src"),
    )
    return jax.shard_map(
        local,
        mesh=mesh,
        in_specs=placed,
        out_specs=(P(("dom", "src"), None), P(("dom", "src"), None)),
        check_vma=False,
    )
```

```python
import functools

import jax
import jax.numpy as jnp
from jax import lax
from jax.experimental import pallas as pl
from jax.experimental.pallas import tpu as pltpu
from jax.sharding import PartitionSpec as P

ROWS = 1024
WIDTH = 256
PART = 4096
EDGES = 8192
CHUNK = 512
UNROLL = 4
SUB = 256
WIN = 384
SPAN = 512
PADDED = PART + WIN
CNT = 16
LOCAL_END = 1 << 22
ACTIVE_END = 1 << 23
F32 = jnp.float32
BF16 = jnp.bfloat16


def in_hbm(x):
    return pltpu.with_memory_space_constraint(x, pltpu.HBM)


def one_hot(mask):
    return jnp.where(mask, 1.0, 0.0).astype(BF16)


def iota(shape, dim):
    return lax.broadcasted_iota(jnp.int32, shape, dim)


def key_column(row):
    return jnp.transpose(jnp.broadcast_to(row, (128, 128)))


def source_of(keys, remote):
    return jnp.where((keys >> 22) == remote, keys & 1023, -1)


def target_of(keys):
    return (keys >> 10) & 4095


def local_edges(keys_s):
    def step(i, lo):
        probe = lo + (4096 >> i)
        return jnp.where(keys_s[probe - 1] < LOCAL_END, probe, lo)

    lo = lax.fori_loop(0, 13, step, 0)
    return jnp.where((lo == EDGES - 1) & (keys_s[EDGES - 1] < LOCAL_END), EDGES, lo)


def edge_range(keys_s, active_s, remote):
    boundary = local_edges(keys_s)
    if remote:
        return boundary, active_s[0] * 128
    return 0, boundary


def sub_range(keys_s, start, lo, hi):
    first = jnp.maximum(start, lo)
    last = jnp.minimum(start + SUB - 1, hi - 1)
    base = (target_of(keys_s[first]) // 16) * 16
    count = jnp.where(last >= first, (target_of(keys_s[last]) - base) // WIN + 1, 0)
    return base, count


def place_of(targets, off):
    return jnp.concatenate([one_hot(iota((WIN, 128), 0) + off == x) for x in targets], axis=1)


def pick_of(rows, remote):
    parts = []
    for row in rows:
        src = source_of(key_column(row), remote)
        parts.append(
            jnp.concatenate([one_hot(src == iota((128, 128), 1) + 128 * c) for c in range(ROWS // 128)], axis=1)
        )
    return jnp.concatenate(parts, axis=0)


def further_windows(todo, run):
    most = todo[0][1]
    for item in todo[1:]:
        most = jnp.maximum(most, item[1])

    @pl.when(most > 1)
    def _():
        for item in todo:

            def window(w, c):
                run(item, pl.multiple_of(item[0] + w * WIN, 16))
                return c

            lax.fori_loop(1, item[1], window, 0)


def tiles(lo, hi, body):
    first = lo // SUB
    count = (hi + SUB - 1) // SUB - first

    def wide(t, carry):
        body(first + t * UNROLL, UNROLL)
        return carry

    def narrow(t, carry):
        body(first + (count // UNROLL) * UNROLL + t, 1)
        return carry

    lax.fori_loop(0, count // UNROLL, wide, 0)
    lax.fori_loop(0, count % UNROLL, narrow, 0)


def aggregate(keys_s, keys_v, table, acc, lo, hi, remote):
    def tile(first_sub, unroll):
        rows = [keys_v[2 * first_sub + j] for j in range(2 * unroll)]
        got = jnp.dot(pick_of(rows, remote), table[...], preferred_element_type=F32).astype(BF16)
        todo = []
        for u in range(unroll):
            base, count = sub_range(keys_s, (first_sub + u) * SUB, lo, hi)
            base = pl.multiple_of(base, 16)
            targets = [target_of(r) for r in rows[2 * u : 2 * u + 2]]
            piece = got[SUB * u : SUB * u + SUB]
            first = jnp.dot(place_of(targets, base), piece, preferred_element_type=F32)
            todo.append((base, count, targets, piece, first))
        for base, count, targets, piece, first in todo:
            acc[pl.ds(base, WIN), :] += first

        def run(item, off):
            acc[pl.ds(off, WIN), :] += jnp.dot(place_of(item[2], off), item[3], preferred_element_type=F32)

        further_windows(todo, run)

    tiles(lo, hi, tile)


def prepare_kernel(keys_s, active_s, keys_v, table_hbm, local_out, counts, table, acc, sems):
    load = pltpu.make_async_copy(table_hbm, table, sems.at[0])
    load.start()
    acc[...] = jnp.zeros_like(acc)
    boundary = local_edges(keys_s)
    load.wait()
    aggregate(keys_s, keys_v, table, acc, 0, boundary, 0)
    save = pltpu.make_async_copy(acc.at[pl.ds(0, PART), :], local_out, sems.at[1])
    save.start()

    def tally(t, total):
        keys = [keys_v[32 * t + j] for j in range(32)]
        high = jnp.concatenate(
            [one_hot((iota((32, 128), 0) == (target_of(k) >> 7)) & (k < ACTIVE_END)) for k in keys], axis=1
        )
        low = jnp.concatenate([one_hot(iota((128, 128), 0) == (target_of(k) & 127)) for k in keys], axis=1)
        return total + lax.dot_general(high, low, (((1,), (1,)), ((), ())), preferred_element_type=F32)

    total = lax.fori_loop(0, EDGES // 4096, tally, jnp.zeros((32, 128), F32))
    upper = jnp.floor(total * (1.0 / 256.0))
    lower = total - upper * 256.0
    for s in range(4):
        both = jnp.concatenate([upper[8 * s : 8 * s + 8], lower[8 * s : 8 * s + 8]], axis=1)
        counts[s] = jnp.concatenate([both, jnp.zeros((8, WIDTH), F32)], axis=0).astype(BF16)
    save.wait()


def forward_remote_kernel(keys_s, active_s, owner_s, keys_v, table, counts, local_hbm, *refs):
    outs, (local_part, acc, sem) = refs[:4], refs[4:]
    load = pltpu.make_async_copy(local_hbm, local_part, sem)
    load.start()
    acc[...] = jnp.zeros_like(acc)
    aggregate(keys_s, keys_v, table, acc, local_edges(keys_s), active_s[0] * 128, 1)
    load.wait()
    for shift, out in enumerate(outs):
        owner = owner_s[shift]
        rows = pl.ds(pl.multiple_of(owner * ROWS, ROWS), ROWS)
        out[:ROWS, :] = (acc[rows, :] + local_part[rows, :]).astype(BF16)
        out[ROWS:, :] = counts[owner]


def transposed_kernel(keys_s, active_s, keys_v, adj):
    adj[...] = jnp.zeros_like(adj)
    lo, hi = local_edges(keys_s), active_s[0] * 128
    blocks = SPAN // 128

    def product(rows, block):
        place = jnp.concatenate([one_hot(iota((ROWS, 128), 0) == source_of(r, 1)) for r in rows], axis=1)
        match = jnp.concatenate(
            [one_hot(iota((SPAN, 128), 0) + block * 128 == target_of(r)) for r in rows], axis=1
        )
        return lax.dot_general(place, match, (((1,), (1,)), ((), ())), preferred_element_type=F32).astype(BF16)

    def add(block, value):
        for k in range(blocks):
            adj[block + k] += value[:, 128 * k : 128 * k + 128]

    def tile(first_sub, unroll):
        todo = []
        for u in range(unroll):
            first = jnp.maximum((first_sub + u) * SUB, lo)
            last = jnp.minimum((first_sub + u) * SUB + SUB - 1, hi - 1)
            block = target_of(keys_s[first]) >> 7
            final = target_of(keys_s[last]) >> 7
            rows = [keys_v[2 * (first_sub + u) + j] for j in range(2)]
            todo.append((block, (final - block) // blocks + 1, rows, product(rows, block)))
        for block, count, rows, value in todo:
            add(block, value)
        most = todo[0][1]
        for item in todo[1:]:
            most = jnp.maximum(most, item[1])

        @pl.when(most > 1)
        def _():
            for block, count, rows, value in todo:

                def window(w, c):
                    add(block + w * blocks, product(rows, block + w * blocks))
                    return c

                lax.fori_loop(1, count, window, 0)

    tiles(lo, hi, tile)


def pick_kernel(senders, table, out, acc):
    for c in range(8):
        col = key_column(senders[c : c + 1, :])
        pick = jnp.concatenate([one_hot(col == iota((128, 128), 1) + 128 * k) for k in range(ROWS // 128)], axis=1)
        acc[:, c, :] = jnp.dot(pick, table[...], preferred_element_type=F32)
    out[...] = acc[...].astype(BF16)


def combine_kernel(senders, returned, kept, out_hbm, out, sems):
    saves = []
    for i in range(4):
        rows = pl.ds(i * (ROWS // 4), ROWS // 4)
        nodes = iota((ROWS // 4, 128), 0) + i * (ROWS // 4)
        place = jnp.concatenate([one_hot(nodes == senders[j]) for j in range(ROWS // 128)], axis=1)
        out[rows, :] = kept[rows, :] + jnp.dot(place, returned[...], preferred_element_type=F32)
        saves.append(pltpu.make_async_copy(out.at[rows, :], out_hbm.at[rows, :], sems.at[i]))
        saves[i].start()
    for copy in saves:
        copy.wait()


def dense_kernel(feats, cots, w_self, w_neigh, bias, *refs):
    parts, counts, (acts, scaled, up_out, inv_ref) = refs[:4], refs[4:8], refs[8:]
    i = pl.program_id(0)

    @pl.when(i == 0)
    def _():
        deg = jnp.zeros((8, 128), F32)
        for s in range(4):
            c = counts[s][...].astype(F32)
            deg = deg + c[:8, :128] * 256.0 + c[:8, 128:]
        inv = 1.0 / jnp.maximum(deg, 1.0)
        for r in range(8):
            inv_ref[r] = inv[r : r + 1]

    cols = [key_column(inv_ref[2 * i + r]) for r in range(2)]
    inverse = jnp.concatenate([jnp.concatenate([c, c], axis=1) for c in cols], axis=0)
    totals = parts[0][...].astype(F32)
    for s in range(1, 4):
        totals = totals + parts[s][...].astype(F32)
    mean = (totals * inverse).astype(BF16)
    pre = (
        jnp.dot(feats[...], w_self[...], preferred_element_type=F32)
        + jnp.dot(mean, w_neigh[...], preferred_element_type=F32)
        + bias[...].astype(F32)
    )
    sigma = jax.nn.sigmoid(pre)
    acts[...] = (pre * sigma).astype(BF16)
    slope = sigma * (1.0 + pre * (1.0 - sigma))
    up = (cots[...].astype(F32) * slope).astype(BF16)
    back = lax.dot_general(up, w_neigh[...], (((1,), (1,)), ((), ())), preferred_element_type=F32)
    scaled[...] = (back * inverse).astype(BF16)
    up_out[...] = up


def scatter_back(keys_s, active_s, keys_v, spread, rows_ref, acc, remote):
    lo, hi = edge_range(keys_s, active_s, remote)

    def tile(t, carry):
        rows = [keys_v[4 * t + j] for j in range(4)]
        for sub in range(CHUNK // SUB):
            base, count = sub_range(keys_s, t * CHUNK + sub * SUB, lo, hi)
            cols = [target_of(key_column(rows[2 * sub + j])) for j in range(2)]

            def window(w):
                off = pl.multiple_of(base + w * WIN, 16)
                pick = jnp.concatenate(
                    [
                        jnp.concatenate(
                            [one_hot(c - off == iota((128, 128), 1) + 128 * k) for k in range(WIN // 128)], axis=1
                        )
                        for c in cols
                    ],
                    axis=0,
                )
                return jnp.dot(pick, spread[pl.ds(off, WIN), :], preferred_element_type=F32)

            rows_ref[sub * SUB : (sub + 1) * SUB, :] = window(0)

            def more(w, c):
                rows_ref[sub * SUB : (sub + 1) * SUB, :] += window(w)
                return c

            lax.fori_loop(1, count, more, 0)
        place = jnp.concatenate(
            [one_hot(iota((ROWS, 128), 0) == source_of(rows[j], remote)) for j in range(4)], axis=1
        )
        acc[...] += jnp.dot(place, rows_ref[...].astype(BF16), preferred_element_type=F32)
        return carry

    lax.fori_loop(lo // CHUNK, (hi + CHUNK - 1) // CHUNK, tile, 0)


def piece_sum(owner_s, pieces, adj, start):
    total = start
    for shift, piece in pieces:
        for h in range(ROWS // SUB):
            block = owner_s[shift] * (ROWS // 128) + 2 * h
            both = jnp.concatenate([adj[block], adj[block + 1]], axis=1)
            part = jnp.dot(both, piece[h * SUB : h * SUB + SUB, :], preferred_element_type=F32)
            total = part if total is None else total + part
    return total


def backward_near_kernel(owner_s, own, left, right, adj, out):
    out[...] = piece_sum(owner_s, ((0, own), (3, left), (1, right)), adj, None)


def backward_far_kernel(owner_s, far, near, adj, out):
    out[...] = piece_sum(owner_s, ((2, far),), adj, near[...]).astype(BF16)


def backward_local_kernel(keys_s, active_s, owner_s, keys_v, up, w_self, p0, p1, p2, p3, out, spread, rows_ref, sems):
    loads = []
    for n, (shift, piece) in enumerate(((0, p0), (3, p1), (1, p2), (2, p3))):
        rows = pl.ds(pl.multiple_of(owner_s[shift] * ROWS, ROWS), ROWS)
        loads.append(pltpu.make_async_copy(piece, spread.at[rows, :], sems.at[n]))
        loads[n].start()
    spread[PART:, :] = jnp.zeros((WIN, WIDTH), BF16)
    out[...] = lax.dot_general(up[...], w_self[...], (((1,), (1,)), ((), ())), preferred_element_type=F32)
    for copy in loads:
        copy.wait()
    scatter_back(keys_s, active_s, keys_v, spread, rows_ref, out, 0)


VMEM = pl.BlockSpec(memory_space=pltpu.VMEM)
ANY = pl.BlockSpec(memory_space=pl.ANY)
HBM = pl.BlockSpec(memory_space=pltpu.HBM)
def params(mib):
    return pltpu.CompilerParams(vmem_limit_bytes=mib << 20)


def local(features, cotangent, w_self, w_neigh, bias, send_rows, edge_src, edge_dst, tile_count):
    peers, capacity = send_rows.shape[2], send_rows.shape[3]
    shape = jax.ShapeDtypeStruct
    picked = pl.pallas_call(
        pick_kernel,
        grid=(1,),
        in_specs=[
            pl.BlockSpec((capacity, peers), lambda i: (0, 0)),
            pl.BlockSpec((ROWS, WIDTH), lambda i: (0, 0)),
        ],
        out_specs=pl.BlockSpec((peers, capacity, WIDTH), lambda i: (0, 0, 0)),
        out_shape=shape((peers, capacity, WIDTH), BF16),
        scratch_shapes=[pltpu.VMEM((peers, capacity, WIDTH), F32)],
        compiler_params=params(8),
        name="pick_rows",
    )(in_hbm(jnp.transpose(send_rows.reshape(peers, capacity))), in_hbm(features))
    remote = lax.all_to_all(picked, "dom", split_axis=0, concat_axis=0, tiled=True).reshape(peers * capacity, WIDTH)

    sources = edge_src.reshape(EDGES)
    targets = edge_dst.reshape(EDGES)
    active = tile_count.reshape(1)
    live = jnp.arange(EDGES, dtype=jnp.int32) < active[0] * 128
    keys = ((sources >> 10) << 22) + (targets << 10) + (sources & 1023)
    keys_s = lax.sort(jnp.where(live, keys, ACTIVE_END))
    keys_v = keys_s.reshape(EDGES // 128, 1, 128)

    before, counts = pl.pallas_call(
        prepare_kernel,
        grid_spec=pltpu.PrefetchScalarGridSpec(
            num_scalar_prefetch=2,
            grid=(),
            in_specs=[VMEM, HBM],
            out_specs=(HBM, VMEM),
            scratch_shapes=[
                pltpu.VMEM((ROWS, WIDTH), BF16),
                pltpu.VMEM((PADDED, WIDTH), F32),
                pltpu.SemaphoreType.DMA((2,)),
            ],
        ),
        out_shape=(pltpu.HBM((PART, WIDTH), F32), shape((4, CNT, WIDTH), BF16)),
        compiler_params=params(20),
        name="prepare",
    )(keys_s, active, keys_v, in_hbm(features))
    rank = lax.axis_index("src")
    order = lax.optimization_barrier((rank + jnp.arange(4, dtype=jnp.int32)) % 4)

    def shifted(x, k):
        return lax.ppermute(x, "src", [(j, (j + k) % 4) for j in range(4)])

    partial_own, partial_next, partial_far, partial_prev = pl.pallas_call(
        forward_remote_kernel,
        grid_spec=pltpu.PrefetchScalarGridSpec(
            num_scalar_prefetch=3,
            grid=(),
            in_specs=[VMEM, VMEM, VMEM, HBM],
            out_specs=[VMEM] * 4,
            scratch_shapes=[
                pltpu.VMEM((PART, WIDTH), F32),
                pltpu.VMEM((PADDED, WIDTH), F32),
                pltpu.SemaphoreType.DMA,
            ],
        ),
        out_shape=[shape((ROWS + CNT, WIDTH), BF16)] * 4,
        compiler_params=params(24),
        name="aggregate_remote",
    )(keys_s, active, order, keys_v, remote, counts, in_hbm(before))
    from_far = shifted(partial_far, 2)
    from_prev = shifted(partial_next, 1)
    from_next = shifted(partial_prev, 3)
    keys_s, partial_own = lax.optimization_barrier((keys_s, partial_own))
    adj_t = pl.pallas_call(
        transposed_kernel,
        grid_spec=pltpu.PrefetchScalarGridSpec(num_scalar_prefetch=2, grid=(), in_specs=[VMEM], out_specs=VMEM),
        out_shape=shape(((PART + SPAN) // 128, ROWS, 128), BF16),
        compiler_params=params(10),
        name="adjacency_transposed",
    )(keys_s, active, keys_v)
    adj_t, from_next = lax.optimization_barrier((adj_t, from_next))
    block = ROWS // 4
    tile = pl.BlockSpec((block, WIDTH), lambda i: (i, 0))
    whole = pl.BlockSpec((WIDTH, WIDTH), lambda i: (0, 0))
    count_rows = pl.BlockSpec((CNT, WIDTH), lambda i: (ROWS // CNT, 0))
    received = (partial_own, from_prev, from_next, from_far)
    acts, scaled, up = pl.pallas_call(
        dense_kernel,
        grid=(4,),
        in_specs=[tile, tile, whole, whole, pl.BlockSpec((1, WIDTH), lambda i: (0, 0))]
        + [tile] * 4
        + [count_rows] * 4,
        out_specs=(tile, tile, tile),
        out_shape=(shape((ROWS, WIDTH), BF16), pltpu.HBM((ROWS, WIDTH), BF16), pltpu.HBM((ROWS, WIDTH), BF16)),
        scratch_shapes=[pltpu.VMEM((8, 1, 128), F32)],
        compiler_params=params(10),
        name="dense_layer",
    )(features, in_hbm(cotangent), w_self, w_neigh, bias.reshape(1, WIDTH), *received, *received)
    far = shifted(scaled, 2)
    prev = shifted(scaled, 1)
    follow = shifted(scaled, 3)

    def backward(kernel, pieces, dtype, name):
        return pl.pallas_call(
            kernel,
            grid_spec=pltpu.PrefetchScalarGridSpec(
                num_scalar_prefetch=1, grid=(), in_specs=[VMEM] * (len(pieces) + 1), out_specs=VMEM
            ),
            out_shape=shape((ROWS, WIDTH), dtype),
            compiler_params=params(8),
            name=name,
        )(order, *pieces, adj_t)

    near = backward(backward_near_kernel, (scaled, prev, follow), F32, "scatter_near")
    outgoing = backward(backward_far_kernel, (far, near), BF16, "scatter_far")
    returned = lax.all_to_all(
        outgoing.reshape(peers, capacity, WIDTH), "dom", split_axis=0, concat_axis=0, tiled=True
    ).reshape(peers * capacity, WIDTH)
    kept = pl.pallas_call(
        backward_local_kernel,
        grid_spec=pltpu.PrefetchScalarGridSpec(
            num_scalar_prefetch=3,
            grid=(),
            in_specs=[VMEM] * 3 + [ANY] * 4,
            out_specs=VMEM,
            scratch_shapes=[
                pltpu.VMEM((PADDED, WIDTH), BF16),
                pltpu.VMEM((CHUNK, WIDTH), F32),
                pltpu.SemaphoreType.DMA((4,)),
            ],
        ),
        out_shape=shape((ROWS, WIDTH), F32),
        compiler_params=params(10),
        name="scatter_local",
    )(keys_s, active, order, keys_v, up, w_self, scaled, prev, follow, far)
    total = pl.pallas_call(
        combine_kernel,
        in_specs=[VMEM] * 3,
        out_specs=HBM,
        out_shape=pltpu.HBM((ROWS, WIDTH), F32),
        scratch_shapes=[pltpu.VMEM((ROWS, WIDTH), F32), pltpu.SemaphoreType.DMA((4,))],
        compiler_params=params(8),
        name="combine",
    )(send_rows.reshape(peers * capacity // 128, 1, 128), returned, kept)
    return acts, total


def solution(mesh):
    placed = (
        P(("dom", "src"), None),
        P(("dom", "src"), None),
        P(),
        P(),
        P(),
        P("dom", "src", None, None),
        P("dom", "src", None),
        P("dom", "src", None),
        P("dom", "src"),
    )
    return jax.shard_map(
        local,
        mesh=mesh,
        in_specs=placed,
        out_specs=(P(("dom", "src"), None), P(("dom", "src"), None)),
        check_vma=False,
    )
```

```python
import functools

import jax
import jax.numpy as jnp
from jax import lax
from jax.experimental import pallas as pl
from jax.experimental.pallas import tpu as pltpu
from jax.sharding import PartitionSpec as P

ROWS = 1024
WIDTH = 256
PART = 4096
EDGES = 8192
CHUNK = 512
UNROLL = 4
SUB = 256
WIN = 384
PADDED = PART + WIN
CNT = 16
LOCAL_END = 1 << 22
ACTIVE_END = 1 << 23
F32 = jnp.float32
BF16 = jnp.bfloat16


def in_hbm(x):
    return pltpu.with_memory_space_constraint(x, pltpu.HBM)


def one_hot(mask):
    return jnp.where(mask, 1.0, 0.0).astype(BF16)


def iota(shape, dim):
    return lax.broadcasted_iota(jnp.int32, shape, dim)


def key_column(row):
    return jnp.transpose(jnp.broadcast_to(row, (128, 128)))


def source_of(keys, remote):
    return jnp.where((keys >> 22) == remote, keys & 1023, -1)


def target_of(keys):
    return (keys >> 10) & 4095


def local_edges(keys_s):
    def step(i, lo):
        probe = lo + (4096 >> i)
        return jnp.where(keys_s[probe - 1] < LOCAL_END, probe, lo)

    lo = lax.fori_loop(0, 13, step, 0)
    return jnp.where((lo == EDGES - 1) & (keys_s[EDGES - 1] < LOCAL_END), EDGES, lo)


def edge_range(keys_s, active_s, remote):
    boundary = local_edges(keys_s)
    if remote:
        return boundary, active_s[0] * 128
    return 0, boundary


def sub_range(keys_s, start, lo, hi):
    first = jnp.maximum(start, lo)
    last = jnp.minimum(start + SUB - 1, hi - 1)
    base = (target_of(keys_s[first]) // 16) * 16
    count = jnp.where(last >= first, (target_of(keys_s[last]) - base) // WIN + 1, 0)
    return base, count


def place_of(targets, off):
    return jnp.concatenate([one_hot(iota((WIN, 128), 0) + off == x) for x in targets], axis=1)


def pick_of(rows, remote):
    parts = []
    for row in rows:
        src = source_of(key_column(row), remote)
        parts.append(
            jnp.concatenate([one_hot(src == iota((128, 128), 1) + 128 * c) for c in range(ROWS // 128)], axis=1)
        )
    return jnp.concatenate(parts, axis=0)


def further_windows(todo, run):
    most = todo[0][1]
    for item in todo[1:]:
        most = jnp.maximum(most, item[1])

    @pl.when(most > 1)
    def _():
        for item in todo:

            def window(w, c):
                run(item, pl.multiple_of(item[0] + w * WIN, 16))
                return c

            lax.fori_loop(1, item[1], window, 0)


def tiles(lo, hi, body):
    first = lo // SUB
    count = (hi + SUB - 1) // SUB - first

    def wide(t, carry):
        body(first + t * UNROLL, UNROLL)
        return carry

    def narrow(t, carry):
        body(first + (count // UNROLL) * UNROLL + t, 1)
        return carry

    lax.fori_loop(0, count // UNROLL, wide, 0)
    lax.fori_loop(0, count % UNROLL, narrow, 0)


def build_adjacency(keys_s, keys_v, adj, lo, hi):
    def tile(first_sub, unroll):
        todo = []
        for u in range(unroll):
            rows = [keys_v[2 * (first_sub + u) + j] for j in range(2)]
            base, count = sub_range(keys_s, (first_sub + u) * SUB, lo, hi)
            base = pl.multiple_of(base, 16)
            targets = [target_of(r) for r in rows]
            first = jnp.dot(place_of(targets, base), pick_of(rows, 1), preferred_element_type=F32).astype(BF16)
            todo.append((base, count, targets, rows, first))
        for base, count, targets, rows, first in todo:
            adj[pl.ds(base, WIN), :] += first

        def run(item, off):
            more = jnp.dot(place_of(item[2], off), pick_of(item[3], 1), preferred_element_type=F32)
            adj[pl.ds(off, WIN), :] += more.astype(BF16)

        further_windows(todo, run)

    tiles(lo, hi, tile)


def aggregate_local(keys_s, keys_v, table, acc, lo, hi):
    def tile(first_sub, unroll):
        rows = [keys_v[2 * first_sub + j] for j in range(2 * unroll)]
        got = jnp.dot(pick_of(rows, 0), table[...], preferred_element_type=F32).astype(BF16)
        todo = []
        for u in range(unroll):
            base, count = sub_range(keys_s, (first_sub + u) * SUB, lo, hi)
            base = pl.multiple_of(base, 16)
            targets = [target_of(r) for r in rows[2 * u : 2 * u + 2]]
            piece = got[SUB * u : SUB * u + SUB]
            first = jnp.dot(place_of(targets, base), piece, preferred_element_type=F32)
            todo.append((base, count, targets, piece, first))
        for base, count, targets, piece, first in todo:
            acc[pl.ds(base, WIN), :] += first

        def run(item, off):
            acc[pl.ds(off, WIN), :] += jnp.dot(place_of(item[2], off), item[3], preferred_element_type=F32)

        further_windows(todo, run)

    tiles(lo, hi, tile)


def prepare_kernel(keys_s, active_s, keys_v, table_hbm, adj_out, local_out, counts, adj, acc, table, sems):
    load = pltpu.make_async_copy(table_hbm, table, sems.at[2])
    load.start()
    boundary = local_edges(keys_s)
    adj[...] = jnp.zeros_like(adj)
    build_adjacency(keys_s, keys_v, adj, boundary, active_s[0] * 128)
    save_adj = pltpu.make_async_copy(adj.at[pl.ds(0, PART), :], adj_out, sems.at[0])
    save_adj.start()
    acc[...] = jnp.zeros_like(acc)
    load.wait()
    aggregate_local(keys_s, keys_v, table, acc, 0, boundary)
    save_acc = pltpu.make_async_copy(acc.at[pl.ds(0, PART), :], local_out, sems.at[1])
    save_acc.start()

    def tally(t, total):
        keys = [keys_v[32 * t + j] for j in range(32)]
        high = jnp.concatenate(
            [one_hot((iota((32, 128), 0) == (target_of(k) >> 7)) & (k < ACTIVE_END)) for k in keys], axis=1
        )
        low = jnp.concatenate([one_hot(iota((128, 128), 0) == (target_of(k) & 127)) for k in keys], axis=1)
        return total + lax.dot_general(high, low, (((1,), (1,)), ((), ())), preferred_element_type=F32)

    total = lax.fori_loop(0, EDGES // 4096, tally, jnp.zeros((32, 128), F32))
    upper = jnp.floor(total * (1.0 / 256.0))
    lower = total - upper * 256.0
    for s in range(4):
        both = jnp.concatenate([upper[8 * s : 8 * s + 8], lower[8 * s : 8 * s + 8]], axis=1)
        counts[s] = jnp.concatenate([both, jnp.zeros((8, WIDTH), F32)], axis=0).astype(BF16)
    save_adj.wait()
    save_acc.wait()


def transpose_kernel(adj, out):
    out[0] = jnp.transpose(adj[...])


def forward_remote_kernel(shifts, owner_s, table, counts, adj_hbm, local_hbm, *refs):
    outs, (adj, local_part, sems) = refs[:-3], refs[-3:]
    halves = ROWS // CHUNK
    loads = []
    for n in range(len(outs)):
        for h in range(halves):
            rows = pl.ds(pl.multiple_of(owner_s[shifts[n]] * ROWS + h * CHUNK, CHUNK), CHUNK)
            i = n * halves + h
            pair = (
                pltpu.make_async_copy(adj_hbm.at[rows, :], adj.at[i], sems.at[0, i]),
                pltpu.make_async_copy(local_hbm.at[rows, :], local_part.at[i], sems.at[1, i]),
            )
            for copy in pair:
                copy.start()
            loads.append(pair)
    for n, out in enumerate(outs):
        out[ROWS:, :] = counts[owner_s[shifts[n]]]
        for h in range(halves):
            i = n * halves + h
            for copy in loads[i]:
                copy.wait()
            total = local_part[i] + jnp.dot(adj[i], table[...], preferred_element_type=F32)
            out[h * CHUNK : h * CHUNK + CHUNK, :] = total.astype(BF16)


def pick_kernel(senders, table, out, acc):
    for c in range(8):
        col = key_column(senders[c : c + 1, :])
        pick = jnp.concatenate([one_hot(col == iota((128, 128), 1) + 128 * k) for k in range(ROWS // 128)], axis=1)
        acc[:, c, :] = jnp.dot(pick, table[...], preferred_element_type=F32)
    out[...] = acc[...].astype(BF16)


def combine_kernel(senders, returned, kept, out_hbm, out, sems):
    saves = []
    for i in range(4):
        rows = pl.ds(i * (ROWS // 4), ROWS // 4)
        nodes = iota((ROWS // 4, 128), 0) + i * (ROWS // 4)
        place = jnp.concatenate([one_hot(nodes == senders[j]) for j in range(ROWS // 128)], axis=1)
        out[rows, :] = kept[rows, :] + jnp.dot(place, returned[...], preferred_element_type=F32)
        saves.append(pltpu.make_async_copy(out.at[rows, :], out_hbm.at[rows, :], sems.at[i]))
        saves[i].start()
    for copy in saves:
        copy.wait()


def dense_kernel(feats, cots, w_self, w_neigh, bias, *refs):
    parts, counts, (acts, scaled, up_out, inv_ref) = refs[:4], refs[4:8], refs[8:]
    i = pl.program_id(0)

    @pl.when(i == 0)
    def _():
        deg = jnp.zeros((8, 128), F32)
        for s in range(4):
            c = counts[s][...].astype(F32)
            deg = deg + c[:8, :128] * 256.0 + c[:8, 128:]
        inv = 1.0 / jnp.maximum(deg, 1.0)
        for r in range(8):
            inv_ref[r] = inv[r : r + 1]

    cols = [key_column(inv_ref[4 * i + r]) for r in range(4)]
    inverse = jnp.concatenate([jnp.concatenate([c, c], axis=1) for c in cols], axis=0)
    totals = parts[0][...].astype(F32)
    for s in range(1, 4):
        totals = totals + parts[s][...].astype(F32)
    mean = (totals * inverse).astype(BF16)
    pre = (
        jnp.dot(feats[...], w_self[...], preferred_element_type=F32)
        + jnp.dot(mean, w_neigh[...], preferred_element_type=F32)
        + bias[...].astype(F32)
    )
    sigma = jax.nn.sigmoid(pre)
    acts[...] = (pre * sigma).astype(BF16)
    slope = sigma * (1.0 + pre * (1.0 - sigma))
    up = (cots[...].astype(F32) * slope).astype(BF16)
    back = lax.dot_general(up, w_neigh[...], (((1,), (1,)), ((), ())), preferred_element_type=F32)
    scaled[...] = (back * inverse).astype(BF16)
    up_out[...] = up


def scatter_back(keys_s, active_s, keys_v, spread, rows_ref, acc, remote):
    lo, hi = edge_range(keys_s, active_s, remote)

    def tile(t, carry):
        rows = [keys_v[4 * t + j] for j in range(4)]
        for sub in range(CHUNK // SUB):
            base, count = sub_range(keys_s, t * CHUNK + sub * SUB, lo, hi)
            cols = [target_of(key_column(rows[2 * sub + j])) for j in range(2)]

            def window(w):
                off = pl.multiple_of(base + w * WIN, 16)
                pick = jnp.concatenate(
                    [
                        jnp.concatenate(
                            [one_hot(c - off == iota((128, 128), 1) + 128 * k) for k in range(WIN // 128)], axis=1
                        )
                        for c in cols
                    ],
                    axis=0,
                )
                return jnp.dot(pick, spread[pl.ds(off, WIN), :], preferred_element_type=F32)

            rows_ref[sub * SUB : (sub + 1) * SUB, :] = window(0)

            def more(w, c):
                rows_ref[sub * SUB : (sub + 1) * SUB, :] += window(w)
                return c

            lax.fori_loop(1, count, more, 0)
        place = jnp.concatenate(
            [one_hot(iota((ROWS, 128), 0) == source_of(rows[j], remote)) for j in range(4)], axis=1
        )
        acc[...] += jnp.dot(place, rows_ref[...].astype(BF16), preferred_element_type=F32)
        return carry

    lax.fori_loop(lo // CHUNK, (hi + CHUNK - 1) // CHUNK, tile, 0)


def piece_sum(owner_s, pieces, adj, start):
    halves = ROWS // CHUNK
    total = start
    for shift, piece in pieces:
        for h in range(halves):
            rows = piece[h * CHUNK : h * CHUNK + CHUNK, :]
            part = jnp.dot(adj[owner_s[shift] * halves + h], rows, preferred_element_type=F32)
            total = part if total is None else total + part
    return total


def backward_near_kernel(owner_s, own, left, right, adj, out):
    out[...] = piece_sum(owner_s, ((0, own), (3, left), (1, right)), adj, None)


def backward_far_kernel(owner_s, far, near, adj, out):
    out[...] = piece_sum(owner_s, ((2, far),), adj, near[...]).astype(BF16)


def backward_local_kernel(keys_s, active_s, owner_s, keys_v, up, w_self, p0, p1, p2, p3, out, spread, rows_ref, sems):
    loads = []
    for n, (shift, piece) in enumerate(((0, p0), (3, p1), (1, p2), (2, p3))):
        rows = pl.ds(pl.multiple_of(owner_s[shift] * ROWS, ROWS), ROWS)
        loads.append(pltpu.make_async_copy(piece, spread.at[rows, :], sems.at[n]))
        loads[n].start()
    spread[PART:, :] = jnp.zeros((WIN, WIDTH), BF16)
    out[...] = lax.dot_general(up[...], w_self[...], (((1,), (1,)), ((), ())), preferred_element_type=F32)
    for copy in loads:
        copy.wait()
    scatter_back(keys_s, active_s, keys_v, spread, rows_ref, out, 0)


VMEM = pl.BlockSpec(memory_space=pltpu.VMEM)
ANY = pl.BlockSpec(memory_space=pl.ANY)
HBM = pl.BlockSpec(memory_space=pltpu.HBM)
def params(mib):
    return pltpu.CompilerParams(vmem_limit_bytes=mib << 20)


def local(features, cotangent, w_self, w_neigh, bias, send_rows, edge_src, edge_dst, tile_count):
    peers, capacity = send_rows.shape[2], send_rows.shape[3]
    shape = jax.ShapeDtypeStruct
    picked = pl.pallas_call(
        pick_kernel,
        grid=(1,),
        in_specs=[
            pl.BlockSpec((capacity, peers), lambda i: (0, 0)),
            pl.BlockSpec((ROWS, WIDTH), lambda i: (0, 0)),
        ],
        out_specs=pl.BlockSpec((peers, capacity, WIDTH), lambda i: (0, 0, 0)),
        out_shape=shape((peers, capacity, WIDTH), BF16),
        scratch_shapes=[pltpu.VMEM((peers, capacity, WIDTH), F32)],
        compiler_params=params(8),
        name="pick_rows",
    )(in_hbm(jnp.transpose(send_rows.reshape(peers, capacity))), in_hbm(features))
    remote = lax.all_to_all(picked, "dom", split_axis=0, concat_axis=0, tiled=True).reshape(peers * capacity, WIDTH)

    sources = edge_src.reshape(EDGES)
    targets = edge_dst.reshape(EDGES)
    active = tile_count.reshape(1)
    live = jnp.arange(EDGES, dtype=jnp.int32) < active[0] * 128
    keys = ((sources >> 10) << 22) + (targets << 10) + (sources & 1023)
    keys_s = lax.sort(jnp.where(live, keys, ACTIVE_END))
    keys_v = keys_s.reshape(EDGES // 128, 1, 128)

    adj, before, counts = pl.pallas_call(
        prepare_kernel,
        grid_spec=pltpu.PrefetchScalarGridSpec(
            num_scalar_prefetch=2,
            grid=(),
            in_specs=[VMEM, HBM],
            out_specs=(HBM, HBM, VMEM),
            scratch_shapes=[
                pltpu.VMEM((PADDED, ROWS), BF16),
                pltpu.VMEM((PADDED, WIDTH), F32),
                pltpu.VMEM((ROWS, WIDTH), BF16),
                pltpu.SemaphoreType.DMA((3,)),
            ],
        ),
        out_shape=(
            pltpu.HBM((PART, ROWS), BF16),
            pltpu.HBM((PART, WIDTH), F32),
            shape((4, CNT, WIDTH), BF16),
        ),
        compiler_params=params(30),
        name="prepare",
    )(keys_s, active, keys_v, in_hbm(features))
    chunks = PART // CHUNK
    rank = lax.axis_index("src")

    order = lax.optimization_barrier((rank + jnp.arange(4, dtype=jnp.int32)) % 4)

    def shifted(x, k):
        return lax.ppermute(x, "src", [(j, (j + k) % 4) for j in range(4)])

    def partials(table, *shifts):
        count = len(shifts)
        return pl.pallas_call(
            functools.partial(forward_remote_kernel, shifts),
            grid_spec=pltpu.PrefetchScalarGridSpec(
                num_scalar_prefetch=1,
                grid=(),
                in_specs=[VMEM, VMEM, HBM, HBM],
                out_specs=[VMEM] * count,
                scratch_shapes=[
                    pltpu.VMEM((2 * count, CHUNK, ROWS), BF16),
                    pltpu.VMEM((2 * count, CHUNK, WIDTH), F32),
                    pltpu.SemaphoreType.DMA((2, 2 * count)),
                ],
            ),
            out_shape=[shape((ROWS + CNT, WIDTH), BF16)] * count,
            compiler_params=params(12),
            name="aggregate_remote_" + "_".join(str(k) for k in shifts),
        )(order, table, counts, in_hbm(adj), in_hbm(before))

    (partial_far,) = partials(remote, 2)
    from_far = shifted(partial_far, 2)
    remote, partial_far = lax.optimization_barrier((remote, partial_far))
    partial_next, partial_prev = partials(remote, 1, 3)
    from_prev = shifted(partial_next, 1)
    from_next = shifted(partial_prev, 3)
    remote, partial = lax.optimization_barrier((remote, partial_next))
    (partial_own,) = partials(remote, 0)
    adj, partial = lax.optimization_barrier((adj, partial))
    adj_t = pl.pallas_call(
        transpose_kernel,
        grid=(chunks,),
        in_specs=[pl.BlockSpec((CHUNK, ROWS), lambda i: (i, 0))],
        out_specs=pl.BlockSpec((1, ROWS, CHUNK), lambda i: (i, 0, 0)),
        out_shape=shape((chunks, ROWS, CHUNK), BF16),
        compiler_params=params(10),
        name="adjacency_transposed",
    )(in_hbm(adj))
    adj_t, from_far = lax.optimization_barrier((adj_t, from_far))

    block = ROWS // 2
    tile = pl.BlockSpec((block, WIDTH), lambda i: (i, 0))
    whole = pl.BlockSpec((WIDTH, WIDTH), lambda i: (0, 0))
    count_rows = pl.BlockSpec((CNT, WIDTH), lambda i: (ROWS // CNT, 0))
    received = (partial_own, from_prev, from_next, from_far)
    acts, scaled, up = pl.pallas_call(
        dense_kernel,
        grid=(2,),
        in_specs=[tile, tile, whole, whole, pl.BlockSpec((1, WIDTH), lambda i: (0, 0))]
        + [tile] * 4
        + [count_rows] * 4,
        out_specs=(tile, tile, tile),
        out_shape=(shape((ROWS, WIDTH), BF16), pltpu.HBM((ROWS, WIDTH), BF16), pltpu.HBM((ROWS, WIDTH), BF16)),
        scratch_shapes=[pltpu.VMEM((8, 1, 128), F32)],
        compiler_params=params(14),
        name="dense_layer",
    )(features, in_hbm(cotangent), w_self, w_neigh, bias.reshape(1, WIDTH), *received, *received)
    far = shifted(scaled, 2)
    prev = shifted(scaled, 1)
    follow = shifted(scaled, 3)

    def backward(kernel, pieces, dtype, name):
        return pl.pallas_call(
            kernel,
            grid_spec=pltpu.PrefetchScalarGridSpec(
                num_scalar_prefetch=1, grid=(), in_specs=[VMEM] * (len(pieces) + 1), out_specs=VMEM
            ),
            out_shape=shape((ROWS, WIDTH), dtype),
            compiler_params=params(8),
            name=name,
        )(order, *pieces, adj_t)

    near = backward(backward_near_kernel, (scaled, prev, follow), F32, "scatter_near")
    outgoing = backward(backward_far_kernel, (far, near), BF16, "scatter_far")
    returned = lax.all_to_all(
        outgoing.reshape(peers, capacity, WIDTH), "dom", split_axis=0, concat_axis=0, tiled=True
    ).reshape(peers * capacity, WIDTH)
    kept = pl.pallas_call(
        backward_local_kernel,
        grid_spec=pltpu.PrefetchScalarGridSpec(
            num_scalar_prefetch=3,
            grid=(),
            in_specs=[VMEM] * 3 + [ANY] * 4,
            out_specs=VMEM,
            scratch_shapes=[
                pltpu.VMEM((PADDED, WIDTH), BF16),
                pltpu.VMEM((CHUNK, WIDTH), F32),
                pltpu.SemaphoreType.DMA((4,)),
            ],
        ),
        out_shape=shape((ROWS, WIDTH), F32),
        compiler_params=params(10),
        name="scatter_local",
    )(keys_s, active, order, keys_v, up, w_self, scaled, prev, follow, far)
    total = pl.pallas_call(
        combine_kernel,
        in_specs=[VMEM] * 3,
        out_specs=HBM,
        out_shape=pltpu.HBM((ROWS, WIDTH), F32),
        scratch_shapes=[pltpu.VMEM((ROWS, WIDTH), F32), pltpu.SemaphoreType.DMA((4,))],
        compiler_params=params(8),
        name="combine",
    )(send_rows.reshape(peers * capacity // 128, 1, 128), returned, kept)
    return acts, total


def solution(mesh):
    placed = (
        P(("dom", "src"), None),
        P(("dom", "src"), None),
        P(),
        P(),
        P(),
        P("dom", "src", None, None),
        P("dom", "src", None),
        P("dom", "src", None),
        P("dom", "src"),
    )
    return jax.shard_map(
        local,
        mesh=mesh,
        in_specs=placed,
        out_specs=(P(("dom", "src"), None), P(("dom", "src"), None)),
        check_vma=False,
    )
```

```python
import functools

import jax
import jax.numpy as jnp
from jax import lax
from jax.experimental import pallas as pl
from jax.experimental.pallas import tpu as pltpu
from jax.sharding import PartitionSpec as P

ROWS = 1024
WIDTH = 256
PART = 4096
EDGES = 8192
CHUNK = 512
UNROLL = 4
SUB = 256
WIN = 320
BACK = 384
FINE = 256
PADDED = PART + BACK
CNT = 16
LOCAL_END = 1 << 22
ACTIVE_END = 1 << 23
F32 = jnp.float32
BF16 = jnp.bfloat16


def in_hbm(x):
    return pltpu.with_memory_space_constraint(x, pltpu.HBM)


def one_hot(mask):
    return jnp.where(mask, 1.0, 0.0).astype(BF16)


def iota(shape, dim):
    return lax.broadcasted_iota(jnp.int32, shape, dim)


def key_column(row):
    return jnp.transpose(jnp.broadcast_to(row, (128, 128)))


def source_of(keys, remote):
    return jnp.where((keys >> 22) == remote, keys & 1023, -1)


def target_of(keys):
    return (keys >> 10) & 4095


def local_edges(keys_s):
    def step(i, lo):
        probe = lo + (4096 >> i)
        return jnp.where(keys_s[probe - 1] < LOCAL_END, probe, lo)

    lo = lax.fori_loop(0, 13, step, 0)
    return jnp.where((lo == EDGES - 1) & (keys_s[EDGES - 1] < LOCAL_END), EDGES, lo)


def edge_range(keys_s, active_s, remote):
    boundary = local_edges(keys_s)
    if remote:
        return boundary, active_s[0] * 128
    return 0, boundary


def sub_range(keys_s, start, lo, hi, win=WIN):
    first = jnp.maximum(start, lo)
    last = jnp.minimum(start + SUB - 1, hi - 1)
    base = (target_of(keys_s[first]) // 16) * 16
    count = jnp.where(last >= first, (target_of(keys_s[last]) - base) // win + 1, 0)
    return base, count


def place_of(targets, off):
    return jnp.concatenate([one_hot(iota((WIN, 128), 0) + off == x) for x in targets], axis=1)


def pick_of(rows, remote):
    parts = []
    for row in rows:
        src = source_of(key_column(row), remote)
        parts.append(
            jnp.concatenate([one_hot(src == iota((128, 128), 1) + 128 * c) for c in range(ROWS // 128)], axis=1)
        )
    return jnp.concatenate(parts, axis=0)


def further_windows(todo, run):
    most = todo[0][1]
    for item in todo[1:]:
        most = jnp.maximum(most, item[1])

    @pl.when(most > 1)
    def _():
        for item in todo:

            def window(w, c):
                run(item, pl.multiple_of(item[0] + w * WIN, 16))
                return c

            lax.fori_loop(1, item[1], window, 0)


def tiles(lo, hi, body):
    first = lo // SUB
    count = (hi + SUB - 1) // SUB - first

    def wide(t, carry):
        body(first + t * UNROLL, UNROLL)
        return carry

    def narrow(t, carry):
        body(first + (count // UNROLL) * UNROLL + t, 1)
        return carry

    lax.fori_loop(0, count // UNROLL, wide, 0)
    lax.fori_loop(0, count % UNROLL, narrow, 0)


def build_adjacency(keys_s, keys_v, adj, lo, hi):
    def tile(first_sub, unroll):
        todo = []
        for u in range(unroll):
            rows = [keys_v[2 * (first_sub + u) + j] for j in range(2)]
            base, count = sub_range(keys_s, (first_sub + u) * SUB, lo, hi)
            base = pl.multiple_of(base, 16)
            targets = [target_of(r) for r in rows]
            first = jnp.dot(place_of(targets, base), pick_of(rows, 1), preferred_element_type=F32).astype(BF16)
            todo.append((base, count, targets, rows, first))
        for base, count, targets, rows, first in todo:
            adj[pl.ds(base, WIN), :] += first

        def run(item, off):
            more = jnp.dot(place_of(item[2], off), pick_of(item[3], 1), preferred_element_type=F32)
            adj[pl.ds(off, WIN), :] += more.astype(BF16)

        further_windows(todo, run)

    tiles(lo, hi, tile)


def aggregate_local(keys_s, keys_v, table, acc, lo, hi):
    def tile(first_sub, unroll):
        rows = [keys_v[2 * first_sub + j] for j in range(2 * unroll)]
        got = jnp.dot(pick_of(rows, 0), table[...], preferred_element_type=F32).astype(BF16)
        todo = []
        for u in range(unroll):
            base, count = sub_range(keys_s, (first_sub + u) * SUB, lo, hi)
            base = pl.multiple_of(base, 16)
            targets = [target_of(r) for r in rows[2 * u : 2 * u + 2]]
            piece = got[SUB * u : SUB * u + SUB]
            first = jnp.dot(place_of(targets, base), piece, preferred_element_type=F32)
            todo.append((base, count, targets, piece, first))
        for base, count, targets, piece, first in todo:
            acc[pl.ds(base, WIN), :] += first

        def run(item, off):
            acc[pl.ds(off, WIN), :] += jnp.dot(place_of(item[2], off), item[3], preferred_element_type=F32)

        further_windows(todo, run)

    tiles(lo, hi, tile)


def prepare_kernel(keys_s, active_s, keys_v, table_hbm, adj_out, local_out, counts, adj, acc, table, sems):
    load = pltpu.make_async_copy(table_hbm, table, sems.at[2])
    load.start()
    boundary = local_edges(keys_s)
    adj[...] = jnp.zeros_like(adj)
    build_adjacency(keys_s, keys_v, adj, boundary, active_s[0] * 128)
    save_adj = pltpu.make_async_copy(adj.at[pl.ds(0, PART), :], adj_out, sems.at[0])
    save_adj.start()
    acc[...] = jnp.zeros_like(acc)
    load.wait()
    aggregate_local(keys_s, keys_v, table, acc, 0, boundary)
    save_acc = pltpu.make_async_copy(acc.at[pl.ds(0, PART), :], local_out, sems.at[1])
    save_acc.start()

    def tally(t, total):
        keys = [keys_v[32 * t + j] for j in range(32)]
        high = jnp.concatenate(
            [one_hot((iota((32, 128), 0) == (target_of(k) >> 7)) & (k < ACTIVE_END)) for k in keys], axis=1
        )
        low = jnp.concatenate([one_hot(iota((128, 128), 0) == (target_of(k) & 127)) for k in keys], axis=1)
        return total + lax.dot_general(high, low, (((1,), (1,)), ((), ())), preferred_element_type=F32)

    total = lax.fori_loop(0, EDGES // 4096, tally, jnp.zeros((32, 128), F32))
    upper = jnp.floor(total * (1.0 / 256.0))
    lower = total - upper * 256.0
    for s in range(4):
        both = jnp.concatenate([upper[8 * s : 8 * s + 8], lower[8 * s : 8 * s + 8]], axis=1)
        counts[s] = jnp.concatenate([both, jnp.zeros((8, WIDTH), F32)], axis=0).astype(BF16)
    save_adj.wait()
    save_acc.wait()


def transpose_kernel(adj, out):
    out[0] = jnp.transpose(adj[...])


def forward_remote_kernel(shifts, owner_s, table, counts, adj_hbm, local_hbm, *refs):
    outs, (adj, local_part, sems) = refs[:-3], refs[-3:]
    halves = ROWS // FINE
    loads = []
    for n in range(len(outs)):
        for h in range(halves):
            rows = pl.ds(pl.multiple_of(owner_s[shifts[n]] * ROWS + h * FINE, FINE), FINE)
            i = n * halves + h
            pair = (
                pltpu.make_async_copy(adj_hbm.at[rows, :], adj.at[i], sems.at[0, i]),
                pltpu.make_async_copy(local_hbm.at[rows, :], local_part.at[i], sems.at[1, i]),
            )
            for copy in pair:
                copy.start()
            loads.append(pair)
    for n, out in enumerate(outs):
        out[ROWS:, :] = counts[owner_s[shifts[n]]]
        for h in range(halves):
            i = n * halves + h
            for copy in loads[i]:
                copy.wait()
            total = local_part[i] + jnp.dot(adj[i], table[...], preferred_element_type=F32)
            out[h * FINE : h * FINE + FINE, :] = total.astype(BF16)


def pick_kernel(senders, table, out, acc):
    for c in range(8):
        col = key_column(senders[c : c + 1, :])
        pick = jnp.concatenate([one_hot(col == iota((128, 128), 1) + 128 * k) for k in range(ROWS // 128)], axis=1)
        acc[:, c, :] = jnp.dot(pick, table[...], preferred_element_type=F32)
    out[...] = acc[...].astype(BF16)


def combine_kernel(senders, returned, kept, out_hbm, out, sems):
    saves = []
    for i in range(4):
        rows = pl.ds(i * (ROWS // 4), ROWS // 4)
        nodes = iota((ROWS // 4, 128), 0) + i * (ROWS // 4)
        place = jnp.concatenate([one_hot(nodes == senders[j]) for j in range(ROWS // 128)], axis=1)
        out[rows, :] = kept[rows, :] + jnp.dot(place, returned[...], preferred_element_type=F32)
        saves.append(pltpu.make_async_copy(out.at[rows, :], out_hbm.at[rows, :], sems.at[i]))
        saves[i].start()
    for copy in saves:
        copy.wait()


def dense_kernel(feats, cots, w_self, w_neigh, bias, *refs):
    parts, counts, (acts, scaled, up_out, inv_ref) = refs[:4], refs[4:8], refs[8:]
    i = pl.program_id(0)

    @pl.when(i == 0)
    def _():
        deg = jnp.zeros((8, 128), F32)
        for s in range(4):
            c = counts[s][...].astype(F32)
            deg = deg + c[:8, :128] * 256.0 + c[:8, 128:]
        inv = 1.0 / jnp.maximum(deg, 1.0)
        for r in range(8):
            inv_ref[r] = inv[r : r + 1]

    cols = [key_column(inv_ref[4 * i + r]) for r in range(4)]
    inverse = jnp.concatenate([jnp.concatenate([c, c], axis=1) for c in cols], axis=0)
    totals = parts[0][...].astype(F32)
    for s in range(1, 4):
        totals = totals + parts[s][...].astype(F32)
    mean = (totals * inverse).astype(BF16)
    pre = (
        jnp.dot(feats[...], w_self[...], preferred_element_type=F32)
        + jnp.dot(mean, w_neigh[...], preferred_element_type=F32)
        + bias[...].astype(F32)
    )
    sigma = jax.nn.sigmoid(pre)
    acts[...] = (pre * sigma).astype(BF16)
    slope = sigma * (1.0 + pre * (1.0 - sigma))
    up = (cots[...].astype(F32) * slope).astype(BF16)
    back = lax.dot_general(up, w_neigh[...], (((1,), (1,)), ((), ())), preferred_element_type=F32)
    scaled[...] = (back * inverse).astype(BF16)
    up_out[...] = up


def scatter_back(keys_s, active_s, keys_v, spread, rows_ref, acc, remote):
    lo, hi = edge_range(keys_s, active_s, remote)

    def tile(t, carry):
        rows = [keys_v[4 * t + j] for j in range(4)]
        for sub in range(CHUNK // SUB):
            base, count = sub_range(keys_s, t * CHUNK + sub * SUB, lo, hi, BACK)
            cols = [target_of(key_column(rows[2 * sub + j])) for j in range(2)]

            def window(w):
                off = pl.multiple_of(base + w * BACK, 16)
                pick = jnp.concatenate(
                    [
                        jnp.concatenate(
                            [one_hot(c - off == iota((128, 128), 1) + 128 * k) for k in range(BACK // 128)], axis=1
                        )
                        for c in cols
                    ],
                    axis=0,
                )
                return jnp.dot(pick, spread[pl.ds(off, BACK), :], preferred_element_type=F32)

            rows_ref[sub * SUB : (sub + 1) * SUB, :] = window(0)

            def more(w, c):
                rows_ref[sub * SUB : (sub + 1) * SUB, :] += window(w)
                return c

            lax.fori_loop(1, count, more, 0)
        place = jnp.concatenate(
            [one_hot(iota((ROWS, 128), 0) == source_of(rows[j], remote)) for j in range(4)], axis=1
        )
        acc[...] += jnp.dot(place, rows_ref[...].astype(BF16), preferred_element_type=F32)
        return carry

    lax.fori_loop(lo // CHUNK, (hi + CHUNK - 1) // CHUNK, tile, 0)


def piece_sum(owner_s, pieces, adj, start):
    halves = ROWS // CHUNK
    total = start
    for shift, piece in pieces:
        for h in range(halves):
            rows = piece[h * CHUNK : h * CHUNK + CHUNK, :]
            part = jnp.dot(adj[owner_s[shift] * halves + h], rows, preferred_element_type=F32)
            total = part if total is None else total + part
    return total


def backward_near_kernel(owner_s, own, left, adj, out):
    out[...] = piece_sum(owner_s, ((0, own), (3, left)), adj, None)


def backward_far_kernel(owner_s, right, far, near, adj, out):
    out[...] = piece_sum(owner_s, ((1, right), (2, far)), adj, near[...]).astype(BF16)


def backward_local_kernel(keys_s, active_s, owner_s, keys_v, up, w_self, p0, p1, p2, p3, out, spread, rows_ref, sems):
    loads = []
    for n, (shift, piece) in enumerate(((0, p0), (3, p1), (1, p2), (2, p3))):
        rows = pl.ds(pl.multiple_of(owner_s[shift] * ROWS, ROWS), ROWS)
        loads.append(pltpu.make_async_copy(piece, spread.at[rows, :], sems.at[n]))
        loads[n].start()
    spread[PART:, :] = jnp.zeros((BACK, WIDTH), BF16)
    out[...] = lax.dot_general(up[...], w_self[...], (((1,), (1,)), ((), ())), preferred_element_type=F32)
    for copy in loads:
        copy.wait()
    scatter_back(keys_s, active_s, keys_v, spread, rows_ref, out, 0)


VMEM = pl.BlockSpec(memory_space=pltpu.VMEM)
ANY = pl.BlockSpec(memory_space=pl.ANY)
HBM = pl.BlockSpec(memory_space=pltpu.HBM)
def params(mib):
    return pltpu.CompilerParams(vmem_limit_bytes=mib << 20)


def local(features, cotangent, w_self, w_neigh, bias, send_rows, edge_src, edge_dst, tile_count):
    peers, capacity = send_rows.shape[2], send_rows.shape[3]
    shape = jax.ShapeDtypeStruct
    picked = pl.pallas_call(
        pick_kernel,
        grid=(1,),
        in_specs=[
            pl.BlockSpec((capacity, peers), lambda i: (0, 0)),
            pl.BlockSpec((ROWS, WIDTH), lambda i: (0, 0)),
        ],
        out_specs=pl.BlockSpec((peers, capacity, WIDTH), lambda i: (0, 0, 0)),
        out_shape=shape((peers, capacity, WIDTH), BF16),
        scratch_shapes=[pltpu.VMEM((peers, capacity, WIDTH), F32)],
        compiler_params=params(8),
        name="pick_rows",
    )(in_hbm(jnp.transpose(send_rows.reshape(peers, capacity))), in_hbm(features))
    remote = lax.all_to_all(picked, "dom", split_axis=0, concat_axis=0, tiled=True).reshape(peers * capacity, WIDTH)

    sources = edge_src.reshape(EDGES)
    targets = edge_dst.reshape(EDGES)
    active = tile_count.reshape(1)
    live = jnp.arange(EDGES, dtype=jnp.int32) < active[0] * 128
    keys = ((sources >> 10) << 22) + (targets << 10) + (sources & 1023)
    keys_s = lax.sort(jnp.where(live, keys, ACTIVE_END))
    keys_v = keys_s.reshape(EDGES // 128, 1, 128)

    adj, before, counts = pl.pallas_call(
        prepare_kernel,
        grid_spec=pltpu.PrefetchScalarGridSpec(
            num_scalar_prefetch=2,
            grid=(),
            in_specs=[VMEM, HBM],
            out_specs=(HBM, HBM, VMEM),
            scratch_shapes=[
                pltpu.VMEM((PADDED, ROWS), BF16),
                pltpu.VMEM((PADDED, WIDTH), F32),
                pltpu.VMEM((ROWS, WIDTH), BF16),
                pltpu.SemaphoreType.DMA((3,)),
            ],
        ),
        out_shape=(
            pltpu.HBM((PART, ROWS), BF16),
            pltpu.HBM((PART, WIDTH), F32),
            shape((4, CNT, WIDTH), BF16),
        ),
        compiler_params=params(30),
        name="prepare",
    )(keys_s, active, keys_v, in_hbm(features))
    chunks = PART // CHUNK
    rank = lax.axis_index("src")

    order = lax.optimization_barrier((rank + jnp.arange(4, dtype=jnp.int32)) % 4)

    def shifted(x, k):
        return lax.ppermute(x, "src", [(j, (j + k) % 4) for j in range(4)])

    def partials(table, *shifts):
        count = len(shifts)
        return pl.pallas_call(
            functools.partial(forward_remote_kernel, shifts),
            grid_spec=pltpu.PrefetchScalarGridSpec(
                num_scalar_prefetch=1,
                grid=(),
                in_specs=[VMEM, VMEM, HBM, HBM],
                out_specs=[VMEM] * count,
                scratch_shapes=[
                    pltpu.VMEM((ROWS // FINE * count, FINE, ROWS), BF16),
                    pltpu.VMEM((ROWS // FINE * count, FINE, WIDTH), F32),
                    pltpu.SemaphoreType.DMA((2, ROWS // FINE * count)),
                ],
            ),
            out_shape=[shape((ROWS + CNT, WIDTH), BF16)] * count,
            compiler_params=params(12),
            name="aggregate_remote_" + "_".join(str(k) for k in shifts),
        )(order, table, counts, in_hbm(adj), in_hbm(before))

    (partial_far,) = partials(remote, 2)
    from_far = shifted(partial_far, 2)
    remote, partial_far = lax.optimization_barrier((remote, partial_far))
    partial_next, partial_prev = partials(remote, 1, 3)
    from_prev = shifted(partial_next, 1)
    from_next = shifted(partial_prev, 3)
    remote, partial = lax.optimization_barrier((remote, partial_next))
    (partial_own,) = partials(remote, 0)
    adj, partial = lax.optimization_barrier((adj, partial))
    adj_t = pl.pallas_call(
        transpose_kernel,
        grid=(chunks,),
        in_specs=[pl.BlockSpec((CHUNK, ROWS), lambda i: (i, 0))],
        out_specs=pl.BlockSpec((1, ROWS, CHUNK), lambda i: (i, 0, 0)),
        out_shape=shape((chunks, ROWS, CHUNK), BF16),
        compiler_params=params(10),
        name="adjacency_transposed",
    )(in_hbm(adj))
    adj_t, from_far = lax.optimization_barrier((adj_t, from_far))

    block = ROWS // 2
    tile = pl.BlockSpec((block, WIDTH), lambda i: (i, 0))
    whole = pl.BlockSpec((WIDTH, WIDTH), lambda i: (0, 0))
    count_rows = pl.BlockSpec((CNT, WIDTH), lambda i: (ROWS // CNT, 0))
    received = (partial_own, from_prev, from_next, from_far)
    acts, scaled, up = pl.pallas_call(
        dense_kernel,
        grid=(2,),
        in_specs=[tile, tile, whole, whole, pl.BlockSpec((1, WIDTH), lambda i: (0, 0))]
        + [tile] * 4
        + [count_rows] * 4,
        out_specs=(tile, tile, tile),
        out_shape=(shape((ROWS, WIDTH), BF16), pltpu.HBM((ROWS, WIDTH), BF16), pltpu.HBM((ROWS, WIDTH), BF16)),
        scratch_shapes=[pltpu.VMEM((8, 1, 128), F32)],
        compiler_params=params(14),
        name="dense_layer",
    )(features, in_hbm(cotangent), w_self, w_neigh, bias.reshape(1, WIDTH), *received, *received)
    far = shifted(scaled, 2)
    prev = shifted(scaled, 1)
    follow = shifted(scaled, 3)

    def backward(kernel, pieces, dtype, name):
        return pl.pallas_call(
            kernel,
            grid_spec=pltpu.PrefetchScalarGridSpec(
                num_scalar_prefetch=1, grid=(), in_specs=[VMEM] * (len(pieces) + 1), out_specs=VMEM
            ),
            out_shape=shape((ROWS, WIDTH), dtype),
            compiler_params=params(8),
            name=name,
        )(order, *pieces, adj_t)

    near = backward(backward_near_kernel, (scaled, prev), F32, "scatter_near")
    outgoing = backward(backward_far_kernel, (follow, far, near), BF16, "scatter_far")
    returned = lax.all_to_all(
        outgoing.reshape(peers, capacity, WIDTH), "dom", split_axis=0, concat_axis=0, tiled=True
    ).reshape(peers * capacity, WIDTH)
    kept = pl.pallas_call(
        backward_local_kernel,
        grid_spec=pltpu.PrefetchScalarGridSpec(
            num_scalar_prefetch=3,
            grid=(),
            in_specs=[VMEM] * 3 + [ANY] * 4,
            out_specs=VMEM,
            scratch_shapes=[
                pltpu.VMEM((PADDED, WIDTH), BF16),
                pltpu.VMEM((CHUNK, WIDTH), F32),
                pltpu.SemaphoreType.DMA((4,)),
            ],
        ),
        out_shape=shape((ROWS, WIDTH), F32),
        compiler_params=params(10),
        name="scatter_local",
    )(keys_s, active, order, keys_v, up, w_self, scaled, prev, follow, far)
    total = pl.pallas_call(
        combine_kernel,
        in_specs=[VMEM] * 3,
        out_specs=HBM,
        out_shape=pltpu.HBM((ROWS, WIDTH), F32),
        scratch_shapes=[pltpu.VMEM((ROWS, WIDTH), F32), pltpu.SemaphoreType.DMA((4,))],
        compiler_params=params(8),
        name="combine",
    )(send_rows.reshape(peers * capacity // 128, 1, 128), returned, kept)
    return acts, total


def solution(mesh):
    placed = (
        P(("dom", "src"), None),
        P(("dom", "src"), None),
        P(),
        P(),
        P(),
        P("dom", "src", None, None),
        P("dom", "src", None),
        P("dom", "src", None),
        P("dom", "src"),
    )
    return jax.shard_map(
        local,
        mesh=mesh,
        in_specs=placed,
        out_specs=(P(("dom", "src"), None), P(("dom", "src"), None)),
        check_vma=False,
    )
```

```python
import functools

import jax
import jax.numpy as jnp
from jax import lax
from jax.experimental import pallas as pl
from jax.experimental.pallas import tpu as pltpu
from jax.sharding import PartitionSpec as P

ROWS = 1024
WIDTH = 256
PART = 4096
EDGES = 8192
CHUNK = 512
UNROLL = 4
SUB = 256
WIN = 320
BACK = 384
FINE = 256
PADDED = PART + BACK
CNT = 16
LOCAL_END = 1 << 22
ACTIVE_END = 1 << 23
F32 = jnp.float32
BF16 = jnp.bfloat16


def in_hbm(x):
    return pltpu.with_memory_space_constraint(x, pltpu.HBM)


def one_hot(mask):
    return jnp.where(mask, 1.0, 0.0).astype(BF16)


def iota(shape, dim):
    return lax.broadcasted_iota(jnp.int32, shape, dim)


def key_column(row):
    return jnp.transpose(jnp.broadcast_to(row, (128, 128)))


def source_of(keys, remote):
    return jnp.where((keys >> 22) == remote, keys & 1023, -1)


def target_of(keys):
    return (keys >> 10) & 4095


def local_edges(keys_s):
    def step(i, lo):
        probe = lo + (4096 >> i)
        return jnp.where(keys_s[probe - 1] < LOCAL_END, probe, lo)

    lo = lax.fori_loop(0, 13, step, 0)
    return jnp.where((lo == EDGES - 1) & (keys_s[EDGES - 1] < LOCAL_END), EDGES, lo)


def edge_range(keys_s, active_s, remote):
    boundary = local_edges(keys_s)
    if remote:
        return boundary, active_s[0] * 128
    return 0, boundary


def sub_range(keys_s, start, lo, hi, win=WIN):
    first = jnp.maximum(start, lo)
    last = jnp.minimum(start + SUB - 1, hi - 1)
    base = (target_of(keys_s[first]) // 16) * 16
    count = jnp.where(last >= first, (target_of(keys_s[last]) - base) // win + 1, 0)
    return base, count


def place_of(targets, off):
    return jnp.concatenate([one_hot(iota((WIN, 128), 0) + off == x) for x in targets], axis=1)


def pick_of(rows, remote):
    parts = []
    for row in rows:
        src = source_of(key_column(row), remote)
        parts.append(
            jnp.concatenate([one_hot(src == iota((128, 128), 1) + 128 * c) for c in range(ROWS // 128)], axis=1)
        )
    return jnp.concatenate(parts, axis=0)


def further_windows(todo, run):
    most = todo[0][1]
    for item in todo[1:]:
        most = jnp.maximum(most, item[1])

    @pl.when(most > 1)
    def _():
        for item in todo:

            def window(w, c):
                run(item, pl.multiple_of(item[0] + w * WIN, 16))
                return c

            lax.fori_loop(1, item[1], window, 0)


def tiles(lo, hi, body):
    first = lo // SUB
    count = (hi + SUB - 1) // SUB - first

    def wide(t, carry):
        body(first + t * UNROLL, UNROLL)
        return carry

    def narrow(t, carry):
        body(first + (count // UNROLL) * UNROLL + t, 1)
        return carry

    lax.fori_loop(0, count // UNROLL, wide, 0)
    lax.fori_loop(0, count % UNROLL, narrow, 0)


def build_adjacency(keys_s, keys_v, adj, lo, hi):
    def tile(first_sub, unroll):
        todo = []
        for u in range(unroll):
            rows = [keys_v[2 * (first_sub + u) + j] for j in range(2)]
            base, count = sub_range(keys_s, (first_sub + u) * SUB, lo, hi)
            base = pl.multiple_of(base, 16)
            targets = [target_of(r) for r in rows]
            first = jnp.dot(place_of(targets, base), pick_of(rows, 1), preferred_element_type=F32).astype(BF16)
            todo.append((base, count, targets, rows, first))
        for base, count, targets, rows, first in todo:
            adj[pl.ds(base, WIN), :] += first

        def run(item, off):
            more = jnp.dot(place_of(item[2], off), pick_of(item[3], 1), preferred_element_type=F32)
            adj[pl.ds(off, WIN), :] += more.astype(BF16)

        further_windows(todo, run)

    tiles(lo, hi, tile)


def aggregate_local(keys_s, keys_v, table, acc, lo, hi):
    def tile(first_sub, unroll):
        rows = [keys_v[2 * first_sub + j] for j in range(2 * unroll)]
        got = jnp.dot(pick_of(rows, 0), table[...], preferred_element_type=F32).astype(BF16)
        todo = []
        for u in range(unroll):
            base, count = sub_range(keys_s, (first_sub + u) * SUB, lo, hi)
            base = pl.multiple_of(base, 16)
            targets = [target_of(r) for r in rows[2 * u : 2 * u + 2]]
            piece = got[SUB * u : SUB * u + SUB]
            first = jnp.dot(place_of(targets, base), piece, preferred_element_type=F32)
            todo.append((base, count, targets, piece, first))
        for base, count, targets, piece, first in todo:
            acc[pl.ds(base, WIN), :] += first

        def run(item, off):
            acc[pl.ds(off, WIN), :] += jnp.dot(place_of(item[2], off), item[3], preferred_element_type=F32)

        further_windows(todo, run)

    tiles(lo, hi, tile)


def prepare_kernel(keys_s, active_s, keys_v, table_hbm, adj_out, local_out, counts, adj, acc, table, sems):
    load = pltpu.make_async_copy(table_hbm, table, sems.at[2])
    load.start()
    boundary = local_edges(keys_s)
    adj[...] = jnp.zeros_like(adj)
    build_adjacency(keys_s, keys_v, adj, boundary, active_s[0] * 128)
    save_adj = pltpu.make_async_copy(adj.at[pl.ds(0, PART), :], adj_out, sems.at[0])
    save_adj.start()
    acc[...] = jnp.zeros_like(acc)
    load.wait()
    aggregate_local(keys_s, keys_v, table, acc, 0, boundary)
    save_acc = pltpu.make_async_copy(acc.at[pl.ds(0, PART), :], local_out, sems.at[1])
    save_acc.start()

    def tally(t, total):
        keys = [keys_v[32 * t + j] for j in range(32)]
        high = jnp.concatenate(
            [one_hot((iota((32, 128), 0) == (target_of(k) >> 7)) & (k < ACTIVE_END)) for k in keys], axis=1
        )
        low = jnp.concatenate([one_hot(iota((128, 128), 0) == (target_of(k) & 127)) for k in keys], axis=1)
        return total + lax.dot_general(high, low, (((1,), (1,)), ((), ())), preferred_element_type=F32)

    total = lax.fori_loop(0, EDGES // 4096, tally, jnp.zeros((32, 128), F32))
    upper = jnp.floor(total * (1.0 / 256.0))
    lower = total - upper * 256.0
    for s in range(4):
        both = jnp.concatenate([upper[8 * s : 8 * s + 8], lower[8 * s : 8 * s + 8]], axis=1)
        counts[s] = jnp.concatenate([both, jnp.zeros((8, WIDTH), F32)], axis=0).astype(BF16)
    save_adj.wait()
    save_acc.wait()


def transpose_kernel(adj, out):
    out[0] = jnp.transpose(adj[...])


def forward_remote_kernel(shifts, owner_s, table, counts, adj_hbm, local_hbm, *refs):
    outs, (adj, local_part, sems) = refs[:-3], refs[-3:]
    halves = ROWS // FINE
    loads = []
    for n in range(len(outs)):
        for h in range(halves):
            rows = pl.ds(pl.multiple_of(owner_s[shifts[n]] * ROWS + h * FINE, FINE), FINE)
            i = n * halves + h
            pair = (
                pltpu.make_async_copy(adj_hbm.at[rows, :], adj.at[i], sems.at[0, i]),
                pltpu.make_async_copy(local_hbm.at[rows, :], local_part.at[i], sems.at[1, i]),
            )
            for copy in pair:
                copy.start()
            loads.append(pair)
    for n, out in enumerate(outs):
        out[ROWS:, :] = counts[owner_s[shifts[n]]]
        for h in range(halves):
            i = n * halves + h
            for copy in loads[i]:
                copy.wait()
            total = local_part[i] + jnp.dot(adj[i], table[...], preferred_element_type=F32)
            out[h * FINE : h * FINE + FINE, :] = total.astype(BF16)


def pick_kernel(senders, table_hbm, out_hbm, table, out, acc, sems):
    load = pltpu.make_async_copy(table_hbm, table, sems.at[0])
    load.start()
    cols = [key_column(senders[c : c + 1, :]) for c in range(8)]
    saves = []
    for h in range(2):
        peers = slice(64 * h, 64 * h + 64)
        picks = [
            jnp.concatenate([one_hot(col[peers] == iota((64, 128), 1) + 128 * k) for k in range(ROWS // 128)], axis=1)
            for col in cols
        ]
        pick = jnp.concatenate(picks, axis=0)
        if h == 0:
            load.wait()
        got = jnp.dot(pick, table[...], preferred_element_type=F32)
        for c in range(8):
            acc[peers, c, :] = got[64 * c : 64 * c + 64]
        out[peers] = acc[peers].astype(BF16)
        half = pl.ds(64 * h, 64)
        saves.append(pltpu.make_async_copy(out.at[half], out_hbm.at[half], sems.at[1 + h]))
        saves[h].start()
    for copy in saves:
        copy.wait()


def combine_kernel(senders, returned, kept, out_hbm, out, sems):
    saves = []
    for i in range(4):
        rows = pl.ds(i * (ROWS // 4), ROWS // 4)
        nodes = iota((ROWS // 4, 128), 0) + i * (ROWS // 4)
        place = jnp.concatenate([one_hot(nodes == senders[j]) for j in range(ROWS // 128)], axis=1)
        out[rows, :] = kept[rows, :] + jnp.dot(place, returned[...], preferred_element_type=F32)
        saves.append(pltpu.make_async_copy(out.at[rows, :], out_hbm.at[rows, :], sems.at[i]))
        saves[i].start()
    for copy in saves:
        copy.wait()


def dense_kernel(feats, cots, w_self, w_neigh, bias, *refs):
    parts, counts, (acts, scaled, up_out, inv_ref) = refs[:4], refs[4:8], refs[8:]
    i = pl.program_id(0)

    @pl.when(i == 0)
    def _():
        deg = jnp.zeros((8, 128), F32)
        for s in range(4):
            c = counts[s][...].astype(F32)
            deg = deg + c[:8, :128] * 256.0 + c[:8, 128:]
        inv = 1.0 / jnp.maximum(deg, 1.0)
        for r in range(8):
            inv_ref[r] = inv[r : r + 1]

    cols = [key_column(inv_ref[4 * i + r]) for r in range(4)]
    inverse = jnp.concatenate([jnp.concatenate([c, c], axis=1) for c in cols], axis=0)
    totals = parts[0][...].astype(F32)
    for s in range(1, 4):
        totals = totals + parts[s][...].astype(F32)
    mean = (totals * inverse).astype(BF16)
    pre = (
        jnp.dot(feats[...], w_self[...], preferred_element_type=F32)
        + jnp.dot(mean, w_neigh[...], preferred_element_type=F32)
        + bias[...].astype(F32)
    )
    sigma = jax.nn.sigmoid(pre)
    acts[...] = (pre * sigma).astype(BF16)
    slope = sigma * (1.0 + pre * (1.0 - sigma))
    up = (cots[...].astype(F32) * slope).astype(BF16)
    back = lax.dot_general(up, w_neigh[...], (((1,), (1,)), ((), ())), preferred_element_type=F32)
    scaled[...] = (back * inverse).astype(BF16)
    up_out[...] = up


def scatter_back(keys_s, active_s, keys_v, spread, rows_ref, acc, remote):
    lo, hi = edge_range(keys_s, active_s, remote)

    def tile(t, carry):
        rows = [keys_v[4 * t + j] for j in range(4)]
        for sub in range(CHUNK // SUB):
            base, count = sub_range(keys_s, t * CHUNK + sub * SUB, lo, hi, BACK)
            cols = [target_of(key_column(rows[2 * sub + j])) for j in range(2)]

            def window(w):
                off = pl.multiple_of(base + w * BACK, 16)
                pick = jnp.concatenate(
                    [
                        jnp.concatenate(
                            [one_hot(c - off == iota((128, 128), 1) + 128 * k) for k in range(BACK // 128)], axis=1
                        )
                        for c in cols
                    ],
                    axis=0,
                )
                return jnp.dot(pick, spread[pl.ds(off, BACK), :], preferred_element_type=F32)

            rows_ref[sub * SUB : (sub + 1) * SUB, :] = window(0)

            def more(w, c):
                rows_ref[sub * SUB : (sub + 1) * SUB, :] += window(w)
                return c

            lax.fori_loop(1, count, more, 0)
        place = jnp.concatenate(
            [one_hot(iota((ROWS, 128), 0) == source_of(rows[j], remote)) for j in range(4)], axis=1
        )
        acc[...] += jnp.dot(place, rows_ref[...].astype(BF16), preferred_element_type=F32)
        return carry

    lax.fori_loop(lo // CHUNK, (hi + CHUNK - 1) // CHUNK, tile, 0)


def piece_sum(owner_s, pieces, adj, start):
    halves = ROWS // CHUNK
    total = start
    for shift, piece in pieces:
        for h in range(halves):
            rows = piece[h * CHUNK : h * CHUNK + CHUNK, :]
            part = jnp.dot(adj[owner_s[shift] * halves + h], rows, preferred_element_type=F32)
            total = part if total is None else total + part
    return total


def backward_near_kernel(owner_s, own, left, adj, out):
    out[...] = piece_sum(owner_s, ((0, own), (3, left)), adj, None)


def backward_far_kernel(owner_s, right, far, near, adj, out):
    out[...] = piece_sum(owner_s, ((1, right), (2, far)), adj, near[...]).astype(BF16)


def backward_local_kernel(keys_s, active_s, owner_s, keys_v, up, w_self, p0, p1, p2, p3, out, spread, rows_ref, sems):
    loads = []
    for n, (shift, piece) in enumerate(((0, p0), (3, p1), (1, p2), (2, p3))):
        rows = pl.ds(pl.multiple_of(owner_s[shift] * ROWS, ROWS), ROWS)
        loads.append(pltpu.make_async_copy(piece, spread.at[rows, :], sems.at[n]))
        loads[n].start()
    spread[PART:, :] = jnp.zeros((BACK, WIDTH), BF16)
    out[...] = lax.dot_general(up[...], w_self[...], (((1,), (1,)), ((), ())), preferred_element_type=F32)
    for copy in loads:
        copy.wait()
    scatter_back(keys_s, active_s, keys_v, spread, rows_ref, out, 0)


VMEM = pl.BlockSpec(memory_space=pltpu.VMEM)
ANY = pl.BlockSpec(memory_space=pl.ANY)
HBM = pl.BlockSpec(memory_space=pltpu.HBM)
def params(mib):
    return pltpu.CompilerParams(vmem_limit_bytes=mib << 20)


def local(features, cotangent, w_self, w_neigh, bias, send_rows, edge_src, edge_dst, tile_count):
    peers, capacity = send_rows.shape[2], send_rows.shape[3]
    shape = jax.ShapeDtypeStruct
    picked = pl.pallas_call(
        pick_kernel,
        grid=(1,),
        in_specs=[pl.BlockSpec((capacity, peers), lambda i: (0, 0)), HBM],
        out_specs=HBM,
        out_shape=pltpu.HBM((peers, capacity, WIDTH), BF16),
        scratch_shapes=[
            pltpu.VMEM((ROWS, WIDTH), BF16),
            pltpu.VMEM((peers, capacity, WIDTH), BF16),
            pltpu.VMEM((peers, capacity, WIDTH), F32),
            pltpu.SemaphoreType.DMA((3,)),
        ],
        compiler_params=params(12),
        name="pick_rows",
    )(in_hbm(jnp.transpose(send_rows.reshape(peers, capacity))), in_hbm(features))
    remote = lax.all_to_all(picked, "dom", split_axis=0, concat_axis=0, tiled=True).reshape(peers * capacity, WIDTH)

    sources = edge_src.reshape(EDGES)
    targets = edge_dst.reshape(EDGES)
    active = tile_count.reshape(1)
    live = jnp.arange(EDGES, dtype=jnp.int32) < active[0] * 128
    keys = ((sources >> 10) << 22) + (targets << 10) + (sources & 1023)
    keys_s = lax.sort(jnp.where(live, keys, ACTIVE_END))
    keys_v = keys_s.reshape(EDGES // 128, 1, 128)

    adj, before, counts = pl.pallas_call(
        prepare_kernel,
        grid_spec=pltpu.PrefetchScalarGridSpec(
            num_scalar_prefetch=2,
            grid=(),
            in_specs=[VMEM, HBM],
            out_specs=(HBM, HBM, VMEM),
            scratch_shapes=[
                pltpu.VMEM((PADDED, ROWS), BF16),
                pltpu.VMEM((PADDED, WIDTH), F32),
                pltpu.VMEM((ROWS, WIDTH), BF16),
                pltpu.SemaphoreType.DMA((3,)),
            ],
        ),
        out_shape=(
            pltpu.HBM((PART, ROWS), BF16),
            pltpu.HBM((PART, WIDTH), F32),
            shape((4, CNT, WIDTH), BF16),
        ),
        compiler_params=params(30),
        name="prepare",
    )(keys_s, active, keys_v, in_hbm(features))
    chunks = PART // CHUNK
    rank = lax.axis_index("src")

    order = lax.optimization_barrier((rank + jnp.arange(4, dtype=jnp.int32)) % 4)

    def shifted(x, k):
        return lax.ppermute(x, "src", [(j, (j + k) % 4) for j in range(4)])

    def partials(table, *shifts):
        count = len(shifts)
        return pl.pallas_call(
            functools.partial(forward_remote_kernel, shifts),
            grid_spec=pltpu.PrefetchScalarGridSpec(
                num_scalar_prefetch=1,
                grid=(),
                in_specs=[VMEM, VMEM, HBM, HBM],
                out_specs=[VMEM] * count,
                scratch_shapes=[
                    pltpu.VMEM((ROWS // FINE * count, FINE, ROWS), BF16),
                    pltpu.VMEM((ROWS // FINE * count, FINE, WIDTH), F32),
                    pltpu.SemaphoreType.DMA((2, ROWS // FINE * count)),
                ],
            ),
            out_shape=[shape((ROWS + CNT, WIDTH), BF16)] * count,
            compiler_params=params(12),
            name="aggregate_remote_" + "_".join(str(k) for k in shifts),
        )(order, table, counts, in_hbm(adj), in_hbm(before))

    (partial_far,) = partials(remote, 2)
    from_far = shifted(partial_far, 2)
    remote, partial_far = lax.optimization_barrier((remote, partial_far))
    partial_next, partial_prev = partials(remote, 1, 3)
    from_prev = shifted(partial_next, 1)
    from_next = shifted(partial_prev, 3)
    remote, partial = lax.optimization_barrier((remote, partial_next))
    (partial_own,) = partials(remote, 0)
    adj, partial = lax.optimization_barrier((adj, partial))
    adj_t = pl.pallas_call(
        transpose_kernel,
        grid=(chunks,),
        in_specs=[pl.BlockSpec((CHUNK, ROWS), lambda i: (i, 0))],
        out_specs=pl.BlockSpec((1, ROWS, CHUNK), lambda i: (i, 0, 0)),
        out_shape=shape((chunks, ROWS, CHUNK), BF16),
        compiler_params=params(10),
        name="adjacency_transposed",
    )(in_hbm(adj))
    adj_t, from_far = lax.optimization_barrier((adj_t, from_far))

    block = ROWS // 2
    tile = pl.BlockSpec((block, WIDTH), lambda i: (i, 0))
    whole = pl.BlockSpec((WIDTH, WIDTH), lambda i: (0, 0))
    count_rows = pl.BlockSpec((CNT, WIDTH), lambda i: (ROWS // CNT, 0))
    received = (partial_own, from_prev, from_next, from_far)
    acts, scaled, up = pl.pallas_call(
        dense_kernel,
        grid=(2,),
        in_specs=[tile, tile, whole, whole, pl.BlockSpec((1, WIDTH), lambda i: (0, 0))]
        + [tile] * 4
        + [count_rows] * 4,
        out_specs=(tile, tile, tile),
        out_shape=(shape((ROWS, WIDTH), BF16), pltpu.HBM((ROWS, WIDTH), BF16), pltpu.HBM((ROWS, WIDTH), BF16)),
        scratch_shapes=[pltpu.VMEM((8, 1, 128), F32)],
        compiler_params=params(14),
        name="dense_layer",
    )(features, in_hbm(cotangent), w_self, w_neigh, bias.reshape(1, WIDTH), *received, *received)
    far = shifted(scaled, 2)
    prev = shifted(scaled, 1)
    follow = shifted(scaled, 3)

    def backward(kernel, pieces, dtype, name):
        return pl.pallas_call(
            kernel,
            grid_spec=pltpu.PrefetchScalarGridSpec(
                num_scalar_prefetch=1, grid=(), in_specs=[VMEM] * (len(pieces) + 1), out_specs=VMEM
            ),
            out_shape=shape((ROWS, WIDTH), dtype),
            compiler_params=params(8),
            name=name,
        )(order, *pieces, adj_t)

    near = backward(backward_near_kernel, (scaled, prev), F32, "scatter_near")
    outgoing = backward(backward_far_kernel, (follow, far, near), BF16, "scatter_far")
    returned = lax.all_to_all(
        outgoing.reshape(peers, capacity, WIDTH), "dom", split_axis=0, concat_axis=0, tiled=True
    ).reshape(peers * capacity, WIDTH)
    kept = pl.pallas_call(
        backward_local_kernel,
        grid_spec=pltpu.PrefetchScalarGridSpec(
            num_scalar_prefetch=3,
            grid=(),
            in_specs=[VMEM] * 3 + [ANY] * 4,
            out_specs=VMEM,
            scratch_shapes=[
                pltpu.VMEM((PADDED, WIDTH), BF16),
                pltpu.VMEM((CHUNK, WIDTH), F32),
                pltpu.SemaphoreType.DMA((4,)),
            ],
        ),
        out_shape=shape((ROWS, WIDTH), F32),
        compiler_params=params(10),
        name="scatter_local",
    )(keys_s, active, order, keys_v, up, w_self, scaled, prev, follow, far)
    total = pl.pallas_call(
        combine_kernel,
        in_specs=[VMEM] * 3,
        out_specs=HBM,
        out_shape=pltpu.HBM((ROWS, WIDTH), F32),
        scratch_shapes=[pltpu.VMEM((ROWS, WIDTH), F32), pltpu.SemaphoreType.DMA((4,))],
        compiler_params=params(8),
        name="combine",
    )(send_rows.reshape(peers * capacity // 128, 1, 128), returned, kept)
    return acts, total


def solution(mesh):
    placed = (
        P(("dom", "src"), None),
        P(("dom", "src"), None),
        P(),
        P(),
        P(),
        P("dom", "src", None, None),
        P("dom", "src", None),
        P("dom", "src", None),
        P("dom", "src"),
    )
    return jax.shard_map(
        local,
        mesh=mesh,
        in_specs=placed,
        out_specs=(P(("dom", "src"), None), P(("dom", "src"), None)),
        check_vma=False,
    )
```

```python
import functools

import jax
import jax.numpy as jnp
from jax import lax
from jax.experimental import pallas as pl
from jax.experimental.pallas import tpu as pltpu
from jax.sharding import PartitionSpec as P

ROWS = 1024
WIDTH = 256
PART = 4096
EDGES = 8192
CHUNK = 512
UNROLL = 4
SUB = 256
WIN = 320
BACK = 384
FINE = 256
PADDED = PART + BACK
CNT = 16
LOCAL_END = 1 << 22
ACTIVE_END = 1 << 23
F32 = jnp.float32
BF16 = jnp.bfloat16


def in_hbm(x):
    return pltpu.with_memory_space_constraint(x, pltpu.HBM)


def one_hot(mask):
    return jnp.where(mask, 1.0, 0.0).astype(BF16)


def iota(shape, dim):
    return lax.broadcasted_iota(jnp.int32, shape, dim)


def key_column(row):
    return jnp.transpose(jnp.broadcast_to(row, (128, 128)))


def source_of(keys, remote):
    return jnp.where((keys >> 22) == remote, keys & 1023, -1)


def target_of(keys):
    return (keys >> 10) & 4095


def local_edges(keys_s):
    def step(i, lo):
        probe = lo + (4096 >> i)
        return jnp.where(keys_s[probe - 1] < LOCAL_END, probe, lo)

    lo = lax.fori_loop(0, 13, step, 0)
    return jnp.where((lo == EDGES - 1) & (keys_s[EDGES - 1] < LOCAL_END), EDGES, lo)


def edge_range(keys_s, active_s, remote):
    boundary = local_edges(keys_s)
    if remote:
        return boundary, active_s[0] * 128
    return 0, boundary


def sub_range(keys_s, start, lo, hi, win=WIN):
    first = jnp.maximum(start, lo)
    last = jnp.minimum(start + SUB - 1, hi - 1)
    base = (target_of(keys_s[first]) // 16) * 16
    count = jnp.where(last >= first, (target_of(keys_s[last]) - base) // win + 1, 0)
    return base, count


def place_of(targets, off):
    return jnp.concatenate([one_hot(iota((WIN, 128), 0) + off == x) for x in targets], axis=1)


def pick_of(rows, remote):
    parts = []
    for row in rows:
        src = source_of(key_column(row), remote)
        parts.append(
            jnp.concatenate([one_hot(src == iota((128, 128), 1) + 128 * c) for c in range(ROWS // 128)], axis=1)
        )
    return jnp.concatenate(parts, axis=0)


def further_windows(todo, run):
    most = todo[0][1]
    for item in todo[1:]:
        most = jnp.maximum(most, item[1])

    @pl.when(most > 1)
    def _():
        for item in todo:

            def window(w, c):
                run(item, pl.multiple_of(item[0] + w * WIN, 16))
                return c

            lax.fori_loop(1, item[1], window, 0)


def tiles(lo, hi, body):
    first = lo // SUB
    count = (hi + SUB - 1) // SUB - first

    def wide(t, carry):
        body(first + t * UNROLL, UNROLL)
        return carry

    def narrow(t, carry):
        body(first + (count // UNROLL) * UNROLL + t, 1)
        return carry

    lax.fori_loop(0, count // UNROLL, wide, 0)
    lax.fori_loop(0, count % UNROLL, narrow, 0)


def build_adjacency(keys_s, keys_v, adj, lo, hi):
    def tile(first_sub, unroll):
        todo = []
        for u in range(unroll):
            rows = [keys_v[2 * (first_sub + u) + j] for j in range(2)]
            base, count = sub_range(keys_s, (first_sub + u) * SUB, lo, hi)
            base = pl.multiple_of(base, 16)
            targets = [target_of(r) for r in rows]
            first = jnp.dot(place_of(targets, base), pick_of(rows, 1), preferred_element_type=F32).astype(BF16)
            todo.append((base, count, targets, rows, first))
        for base, count, targets, rows, first in todo:
            adj[pl.ds(base, WIN), :] += first

        def run(item, off):
            more = jnp.dot(place_of(item[2], off), pick_of(item[3], 1), preferred_element_type=F32)
            adj[pl.ds(off, WIN), :] += more.astype(BF16)

        further_windows(todo, run)

    tiles(lo, hi, tile)


def aggregate_local(keys_s, keys_v, table, acc, lo, hi):
    def tile(first_sub, unroll):
        rows = [keys_v[2 * first_sub + j] for j in range(2 * unroll)]
        got = jnp.dot(pick_of(rows, 0), table[...], preferred_element_type=F32).astype(BF16)
        todo = []
        for u in range(unroll):
            base, count = sub_range(keys_s, (first_sub + u) * SUB, lo, hi)
            base = pl.multiple_of(base, 16)
            targets = [target_of(r) for r in rows[2 * u : 2 * u + 2]]
            piece = got[SUB * u : SUB * u + SUB]
            first = jnp.dot(place_of(targets, base), piece, preferred_element_type=F32)
            todo.append((base, count, targets, piece, first))
        for base, count, targets, piece, first in todo:
            acc[pl.ds(base, WIN), :] += first

        def run(item, off):
            acc[pl.ds(off, WIN), :] += jnp.dot(place_of(item[2], off), item[3], preferred_element_type=F32)

        further_windows(todo, run)

    tiles(lo, hi, tile)


def prepare_kernel(active_s, keys_any, keys_v, table_hbm, adj_out, local_out, counts, adj, acc, table, keys_s, sems):
    scalars = pltpu.make_async_copy(keys_any, keys_s, sems.at[3])
    scalars.start()
    load = pltpu.make_async_copy(table_hbm, table, sems.at[2])
    load.start()
    adj[...] = jnp.zeros_like(adj)
    scalars.wait()
    boundary = local_edges(keys_s)
    build_adjacency(keys_s, keys_v, adj, boundary, active_s[0] * 128)
    save_adj = pltpu.make_async_copy(adj.at[pl.ds(0, PART), :], adj_out, sems.at[0])
    save_adj.start()
    acc[...] = jnp.zeros_like(acc)
    load.wait()
    aggregate_local(keys_s, keys_v, table, acc, 0, boundary)
    save_acc = pltpu.make_async_copy(acc.at[pl.ds(0, PART), :], local_out, sems.at[1])
    save_acc.start()

    def tally(t, total):
        keys = [keys_v[32 * t + j] for j in range(32)]
        high = jnp.concatenate(
            [one_hot((iota((32, 128), 0) == (target_of(k) >> 7)) & (k < ACTIVE_END)) for k in keys], axis=1
        )
        low = jnp.concatenate([one_hot(iota((128, 128), 0) == (target_of(k) & 127)) for k in keys], axis=1)
        return total + lax.dot_general(high, low, (((1,), (1,)), ((), ())), preferred_element_type=F32)

    total = lax.fori_loop(0, EDGES // 4096, tally, jnp.zeros((32, 128), F32))
    upper = jnp.floor(total * (1.0 / 256.0))
    lower = total - upper * 256.0
    for s in range(4):
        both = jnp.concatenate([upper[8 * s : 8 * s + 8], lower[8 * s : 8 * s + 8]], axis=1)
        counts[s] = jnp.concatenate([both, jnp.zeros((8, WIDTH), F32)], axis=0).astype(BF16)
    save_adj.wait()
    save_acc.wait()


def transpose_kernel(adj, out):
    out[0] = jnp.transpose(adj[...])


def forward_remote_kernel(shifts, owner_s, table, counts, adj_hbm, local_hbm, *refs):
    outs, (adj, local_part, sems) = refs[:-3], refs[-3:]
    halves = ROWS // FINE
    loads = []
    for n in range(len(outs)):
        for h in range(halves):
            rows = pl.ds(pl.multiple_of(owner_s[shifts[n]] * ROWS + h * FINE, FINE), FINE)
            i = n * halves + h
            pair = (
                pltpu.make_async_copy(adj_hbm.at[rows, :], adj.at[i], sems.at[0, i]),
                pltpu.make_async_copy(local_hbm.at[rows, :], local_part.at[i], sems.at[1, i]),
            )
            for copy in pair:
                copy.start()
            loads.append(pair)
    for n, out in enumerate(outs):
        out[ROWS:, :] = counts[owner_s[shifts[n]]]
        for h in range(halves):
            i = n * halves + h
            for copy in loads[i]:
                copy.wait()
            total = local_part[i] + jnp.dot(adj[i], table[...], preferred_element_type=F32)
            out[h * FINE : h * FINE + FINE, :] = total.astype(BF16)


def pick_kernel(senders, table, out, acc):
    for c in range(8):
        col = key_column(senders[c : c + 1, :])
        pick = jnp.concatenate([one_hot(col == iota((128, 128), 1) + 128 * k) for k in range(ROWS // 128)], axis=1)
        acc[:, c, :] = jnp.dot(pick, table[...], preferred_element_type=F32)
    out[...] = acc[...].astype(BF16)


def combine_kernel(senders, returned, kept, out_hbm, out, sems):
    saves = []
    for i in range(4):
        rows = pl.ds(i * (ROWS // 4), ROWS // 4)
        nodes = iota((ROWS // 4, 128), 0) + i * (ROWS // 4)
        place = jnp.concatenate([one_hot(nodes == senders[j]) for j in range(ROWS // 128)], axis=1)
        out[rows, :] = kept[rows, :] + jnp.dot(place, returned[...], preferred_element_type=F32)
        saves.append(pltpu.make_async_copy(out.at[rows, :], out_hbm.at[rows, :], sems.at[i]))
        saves[i].start()
    for copy in saves:
        copy.wait()


def dense_kernel(feats, cots, w_self, w_neigh, bias, *refs):
    parts, counts, (acts, scaled, up_out, inv_ref) = refs[:4], refs[4:8], refs[8:]
    i = pl.program_id(0)

    @pl.when(i == 0)
    def _():
        deg = jnp.zeros((8, 128), F32)
        for s in range(4):
            c = counts[s][...].astype(F32)
            deg = deg + c[:8, :128] * 256.0 + c[:8, 128:]
        inv = 1.0 / jnp.maximum(deg, 1.0)
        for r in range(8):
            inv_ref[r] = inv[r : r + 1]

    cols = [key_column(inv_ref[4 * i + r]) for r in range(4)]
    inverse = jnp.concatenate([jnp.concatenate([c, c], axis=1) for c in cols], axis=0)
    totals = parts[0][...].astype(F32)
    for s in range(1, 4):
        totals = totals + parts[s][...].astype(F32)
    mean = (totals * inverse).astype(BF16)
    pre = (
        jnp.dot(feats[...], w_self[...], preferred_element_type=F32)
        + jnp.dot(mean, w_neigh[...], preferred_element_type=F32)
        + bias[...].astype(F32)
    )
    sigma = jax.nn.sigmoid(pre)
    acts[...] = (pre * sigma).astype(BF16)
    slope = sigma * (1.0 + pre * (1.0 - sigma))
    up = (cots[...].astype(F32) * slope).astype(BF16)
    back = lax.dot_general(up, w_neigh[...], (((1,), (1,)), ((), ())), preferred_element_type=F32)
    scaled[...] = (back * inverse).astype(BF16)
    up_out[...] = up


def scatter_back(keys_s, active_s, keys_v, spread, rows_ref, acc, remote):
    lo, hi = edge_range(keys_s, active_s, remote)

    def tile(t, carry):
        rows = [keys_v[4 * t + j] for j in range(4)]
        for sub in range(CHUNK // SUB):
            base, count = sub_range(keys_s, t * CHUNK + sub * SUB, lo, hi, BACK)
            cols = [target_of(key_column(rows[2 * sub + j])) for j in range(2)]

            def window(w):
                off = pl.multiple_of(base + w * BACK, 16)
                pick = jnp.concatenate(
                    [
                        jnp.concatenate(
                            [one_hot(c - off == iota((128, 128), 1) + 128 * k) for k in range(BACK // 128)], axis=1
                        )
                        for c in cols
                    ],
                    axis=0,
                )
                return jnp.dot(pick, spread[pl.ds(off, BACK), :], preferred_element_type=F32)

            rows_ref[sub * SUB : (sub + 1) * SUB, :] = window(0)

            def more(w, c):
                rows_ref[sub * SUB : (sub + 1) * SUB, :] += window(w)
                return c

            lax.fori_loop(1, count, more, 0)
        place = jnp.concatenate(
            [one_hot(iota((ROWS, 128), 0) == source_of(rows[j], remote)) for j in range(4)], axis=1
        )
        acc[...] += jnp.dot(place, rows_ref[...].astype(BF16), preferred_element_type=F32)
        return carry

    lax.fori_loop(lo // CHUNK, (hi + CHUNK - 1) // CHUNK, tile, 0)


def piece_sum(owner_s, pieces, adj, start):
    halves = ROWS // CHUNK
    total = start
    for shift, piece in pieces:
        for h in range(halves):
            rows = piece[h * CHUNK : h * CHUNK + CHUNK, :]
            part = jnp.dot(adj[owner_s[shift] * halves + h], rows, preferred_element_type=F32)
            total = part if total is None else total + part
    return total


def backward_near_kernel(owner_s, own, left, adj, out):
    out[...] = piece_sum(owner_s, ((0, own), (3, left)), adj, None)


def backward_far_kernel(owner_s, right, far, near, adj, out):
    out[...] = piece_sum(owner_s, ((1, right), (2, far)), adj, near[...]).astype(BF16)


def backward_local_kernel(keys_s, active_s, owner_s, keys_v, up, w_self, p0, p1, p2, p3, out, spread, rows_ref, sems):
    loads = []
    for n, (shift, piece) in enumerate(((0, p0), (3, p1), (1, p2), (2, p3))):
        rows = pl.ds(pl.multiple_of(owner_s[shift] * ROWS, ROWS), ROWS)
        loads.append(pltpu.make_async_copy(piece, spread.at[rows, :], sems.at[n]))
        loads[n].start()
    spread[PART:, :] = jnp.zeros((BACK, WIDTH), BF16)
    out[...] = lax.dot_general(up[...], w_self[...], (((1,), (1,)), ((), ())), preferred_element_type=F32)
    for copy in loads:
        copy.wait()
    scatter_back(keys_s, active_s, keys_v, spread, rows_ref, out, 0)


VMEM = pl.BlockSpec(memory_space=pltpu.VMEM)
ANY = pl.BlockSpec(memory_space=pl.ANY)
HBM = pl.BlockSpec(memory_space=pltpu.HBM)
def params(mib):
    return pltpu.CompilerParams(vmem_limit_bytes=mib << 20)


def local(features, cotangent, w_self, w_neigh, bias, send_rows, edge_src, edge_dst, tile_count):
    peers, capacity = send_rows.shape[2], send_rows.shape[3]
    shape = jax.ShapeDtypeStruct
    picked = pl.pallas_call(
        pick_kernel,
        grid=(1,),
        in_specs=[
            pl.BlockSpec((capacity, peers), lambda i: (0, 0)),
            pl.BlockSpec((ROWS, WIDTH), lambda i: (0, 0)),
        ],
        out_specs=pl.BlockSpec((peers, capacity, WIDTH), lambda i: (0, 0, 0)),
        out_shape=shape((peers, capacity, WIDTH), BF16),
        scratch_shapes=[pltpu.VMEM((peers, capacity, WIDTH), F32)],
        compiler_params=params(8),
        name="pick_rows",
    )(in_hbm(jnp.transpose(send_rows.reshape(peers, capacity))), in_hbm(features))
    remote = lax.all_to_all(picked, "dom", split_axis=0, concat_axis=0, tiled=True).reshape(peers * capacity, WIDTH)

    sources = edge_src.reshape(EDGES)
    targets = edge_dst.reshape(EDGES)
    active = tile_count.reshape(1)
    live = jnp.arange(EDGES, dtype=jnp.int32) < active[0] * 128
    keys = ((sources >> 10) << 22) + (targets << 10) + (sources & 1023)
    keys_s = lax.sort(jnp.where(live, keys, ACTIVE_END))
    keys_v = keys_s.reshape(EDGES // 128, 1, 128)

    adj, before, counts = pl.pallas_call(
        prepare_kernel,
        grid_spec=pltpu.PrefetchScalarGridSpec(
            num_scalar_prefetch=1,
            grid=(),
            in_specs=[ANY, VMEM, HBM],
            out_specs=(HBM, HBM, VMEM),
            scratch_shapes=[
                pltpu.VMEM((PADDED, ROWS), BF16),
                pltpu.VMEM((PADDED, WIDTH), F32),
                pltpu.VMEM((ROWS, WIDTH), BF16),
                pltpu.SMEM((EDGES,), jnp.int32),
                pltpu.SemaphoreType.DMA((4,)),
            ],
        ),
        out_shape=(
            pltpu.HBM((PART, ROWS), BF16),
            pltpu.HBM((PART, WIDTH), F32),
            shape((4, CNT, WIDTH), BF16),
        ),
        compiler_params=params(30),
        name="prepare",
    )(active, keys_s, keys_v, in_hbm(features))
    chunks = PART // CHUNK
    rank = lax.axis_index("src")

    order = lax.optimization_barrier((rank + jnp.arange(4, dtype=jnp.int32)) % 4)

    def shifted(x, k):
        return lax.ppermute(x, "src", [(j, (j + k) % 4) for j in range(4)])

    def partials(table, *shifts):
        count = len(shifts)
        return pl.pallas_call(
            functools.partial(forward_remote_kernel, shifts),
            grid_spec=pltpu.PrefetchScalarGridSpec(
                num_scalar_prefetch=1,
                grid=(),
                in_specs=[VMEM, VMEM, HBM, HBM],
                out_specs=[VMEM] * count,
                scratch_shapes=[
                    pltpu.VMEM((ROWS // FINE * count, FINE, ROWS), BF16),
                    pltpu.VMEM((ROWS // FINE * count, FINE, WIDTH), F32),
                    pltpu.SemaphoreType.DMA((2, ROWS // FINE * count)),
                ],
            ),
            out_shape=[shape((ROWS + CNT, WIDTH), BF16)] * count,
            compiler_params=params(12),
            name="aggregate_remote_" + "_".join(str(k) for k in shifts),
        )(order, table, counts, in_hbm(adj), in_hbm(before))

    (partial_far,) = partials(remote, 2)
    from_far = shifted(partial_far, 2)
    remote, partial_far = lax.optimization_barrier((remote, partial_far))
    partial_next, partial_prev = partials(remote, 1, 3)
    from_prev = shifted(partial_next, 1)
    from_next = shifted(partial_prev, 3)
    remote, partial = lax.optimization_barrier((remote, partial_next))
    (partial_own,) = partials(remote, 0)
    adj, partial = lax.optimization_barrier((adj, partial))
    adj_t = pl.pallas_call(
        transpose_kernel,
        grid=(chunks,),
        in_specs=[pl.BlockSpec((CHUNK, ROWS), lambda i: (i, 0))],
        out_specs=pl.BlockSpec((1, ROWS, CHUNK), lambda i: (i, 0, 0)),
        out_shape=shape((chunks, ROWS, CHUNK), BF16),
        compiler_params=params(10),
        name="adjacency_transposed",
    )(in_hbm(adj))
    adj_t, from_far = lax.optimization_barrier((adj_t, from_far))

    block = ROWS // 2
    tile = pl.BlockSpec((block, WIDTH), lambda i: (i, 0))
    whole = pl.BlockSpec((WIDTH, WIDTH), lambda i: (0, 0))
    count_rows = pl.BlockSpec((CNT, WIDTH), lambda i: (ROWS // CNT, 0))
    received = (partial_own, from_prev, from_next, from_far)
    acts, scaled, up = pl.pallas_call(
        dense_kernel,
        grid=(2,),
        in_specs=[tile, tile, whole, whole, pl.BlockSpec((1, WIDTH), lambda i: (0, 0))]
        + [tile] * 4
        + [count_rows] * 4,
        out_specs=(tile, tile, tile),
        out_shape=(shape((ROWS, WIDTH), BF16), pltpu.HBM((ROWS, WIDTH), BF16), pltpu.HBM((ROWS, WIDTH), BF16)),
        scratch_shapes=[pltpu.VMEM((8, 1, 128), F32)],
        compiler_params=params(14),
        name="dense_layer",
    )(features, in_hbm(cotangent), w_self, w_neigh, bias.reshape(1, WIDTH), *received, *received)
    far = shifted(scaled, 2)
    prev = shifted(scaled, 1)
    follow = shifted(scaled, 3)

    def backward(kernel, pieces, dtype, name):
        return pl.pallas_call(
            kernel,
            grid_spec=pltpu.PrefetchScalarGridSpec(
                num_scalar_prefetch=1, grid=(), in_specs=[VMEM] * (len(pieces) + 1), out_specs=VMEM
            ),
            out_shape=shape((ROWS, WIDTH), dtype),
            compiler_params=params(8),
            name=name,
        )(order, *pieces, adj_t)

    near = backward(backward_near_kernel, (scaled, prev), F32, "scatter_near")
    outgoing = backward(backward_far_kernel, (follow, far, near), BF16, "scatter_far")
    returned = lax.all_to_all(
        outgoing.reshape(peers, capacity, WIDTH), "dom", split_axis=0, concat_axis=0, tiled=True
    ).reshape(peers * capacity, WIDTH)
    kept = pl.pallas_call(
        backward_local_kernel,
        grid_spec=pltpu.PrefetchScalarGridSpec(
            num_scalar_prefetch=3,
            grid=(),
            in_specs=[VMEM] * 3 + [ANY] * 4,
            out_specs=VMEM,
            scratch_shapes=[
                pltpu.VMEM((PADDED, WIDTH), BF16),
                pltpu.VMEM((CHUNK, WIDTH), F32),
                pltpu.SemaphoreType.DMA((4,)),
            ],
        ),
        out_shape=shape((ROWS, WIDTH), F32),
        compiler_params=params(10),
        name="scatter_local",
    )(keys_s, active, order, keys_v, up, w_self, scaled, prev, follow, far)
    total = pl.pallas_call(
        combine_kernel,
        in_specs=[VMEM] * 3,
        out_specs=HBM,
        out_shape=pltpu.HBM((ROWS, WIDTH), F32),
        scratch_shapes=[pltpu.VMEM((ROWS, WIDTH), F32), pltpu.SemaphoreType.DMA((4,))],
        compiler_params=params(8),
        name="combine",
    )(send_rows.reshape(peers * capacity // 128, 1, 128), returned, kept)
    return acts, total


def solution(mesh):
    placed = (
        P(("dom", "src"), None),
        P(("dom", "src"), None),
        P(),
        P(),
        P(),
        P("dom", "src", None, None),
        P("dom", "src", None),
        P("dom", "src", None),
        P("dom", "src"),
    )
    return jax.shard_map(
        local,
        mesh=mesh,
        in_specs=placed,
        out_specs=(P(("dom", "src"), None), P(("dom", "src"), None)),
        check_vma=False,
    )
```

```python
import functools

import jax
import jax.numpy as jnp
from jax import lax
from jax.experimental import pallas as pl
from jax.experimental.pallas import tpu as pltpu
from jax.sharding import PartitionSpec as P

ROWS = 1024
WIDTH = 256
PART = 4096
EDGES = 8192
CHUNK = 512
UNROLL = 4
SUB = 256
WIN = 320
BACK = 384
FINE = 256
PADDED = PART + BACK
CNT = 16
LOCAL_END = 1 << 22
ACTIVE_END = 1 << 23
F32 = jnp.float32
BF16 = jnp.bfloat16


def in_hbm(x):
    return pltpu.with_memory_space_constraint(x, pltpu.HBM)


def one_hot(mask):
    return jnp.where(mask, 1.0, 0.0).astype(BF16)


def iota(shape, dim):
    return lax.broadcasted_iota(jnp.int32, shape, dim)


def key_column(row):
    return jnp.transpose(jnp.broadcast_to(row, (128, 128)))


def source_of(keys, remote):
    return jnp.where((keys >> 22) == remote, keys & 1023, -1)


def target_of(keys):
    return (keys >> 10) & 4095


def local_edges(keys_s):
    def step(i, lo):
        probe = lo + (4096 >> i)
        return jnp.where(keys_s[probe - 1] < LOCAL_END, probe, lo)

    lo = lax.fori_loop(0, 13, step, 0)
    return jnp.where((lo == EDGES - 1) & (keys_s[EDGES - 1] < LOCAL_END), EDGES, lo)


def edge_range(keys_s, active_s, remote):
    boundary = local_edges(keys_s)
    if remote:
        return boundary, active_s[0] * 128
    return 0, boundary


def sub_range(keys_s, start, lo, hi, win=WIN):
    first = jnp.maximum(start, lo)
    last = jnp.minimum(start + SUB - 1, hi - 1)
    base = (target_of(keys_s[first]) // 16) * 16
    count = jnp.where(last >= first, (target_of(keys_s[last]) - base) // win + 1, 0)
    return base, count


def place_of(targets, off):
    return jnp.concatenate([one_hot(iota((WIN, 128), 0) + off == x) for x in targets], axis=1)


def pick_of(rows, remote):
    parts = []
    for row in rows:
        src = source_of(key_column(row), remote)
        parts.append(
            jnp.concatenate([one_hot(src == iota((128, 128), 1) + 128 * c) for c in range(ROWS // 128)], axis=1)
        )
    return jnp.concatenate(parts, axis=0)


def further_windows(todo, run):
    most = todo[0][1]
    for item in todo[1:]:
        most = jnp.maximum(most, item[1])

    @pl.when(most > 1)
    def _():
        for item in todo:

            def window(w, c):
                run(item, pl.multiple_of(item[0] + w * WIN, 16))
                return c

            lax.fori_loop(1, item[1], window, 0)


def tiles(lo, hi, body):
    first = lo // SUB
    count = (hi + SUB - 1) // SUB - first

    def wide(t, carry):
        body(first + t * UNROLL, UNROLL)
        return carry

    def narrow(t, carry):
        body(first + (count // UNROLL) * UNROLL + t, 1)
        return carry

    lax.fori_loop(0, count // UNROLL, wide, 0)
    lax.fori_loop(0, count % UNROLL, narrow, 0)


def build_adjacency(keys_s, keys_v, adj, lo, hi):
    def tile(first_sub, unroll):
        todo = []
        for u in range(unroll):
            rows = [keys_v[2 * (first_sub + u) + j] for j in range(2)]
            base, count = sub_range(keys_s, (first_sub + u) * SUB, lo, hi)
            base = pl.multiple_of(base, 16)
            targets = [target_of(r) for r in rows]
            first = jnp.dot(place_of(targets, base), pick_of(rows, 1), preferred_element_type=F32).astype(BF16)
            todo.append((base, count, targets, rows, first))
        for base, count, targets, rows, first in todo:
            adj[pl.ds(base, WIN), :] += first

        def run(item, off):
            more = jnp.dot(place_of(item[2], off), pick_of(item[3], 1), preferred_element_type=F32)
            adj[pl.ds(off, WIN), :] += more.astype(BF16)

        further_windows(todo, run)

    tiles(lo, hi, tile)


def aggregate_local(keys_s, keys_v, table, acc, lo, hi):
    def tile(first_sub, unroll):
        rows = [keys_v[2 * first_sub + j] for j in range(2 * unroll)]
        got = jnp.dot(pick_of(rows, 0), table[...], preferred_element_type=F32).astype(BF16)
        todo = []
        for u in range(unroll):
            base, count = sub_range(keys_s, (first_sub + u) * SUB, lo, hi)
            base = pl.multiple_of(base, 16)
            targets = [target_of(r) for r in rows[2 * u : 2 * u + 2]]
            piece = got[SUB * u : SUB * u + SUB]
            first = jnp.dot(place_of(targets, base), piece, preferred_element_type=F32)
            todo.append((base, count, targets, piece, first))
        for base, count, targets, piece, first in todo:
            acc[pl.ds(base, WIN), :] += first

        def run(item, off):
            acc[pl.ds(off, WIN), :] += jnp.dot(place_of(item[2], off), item[3], preferred_element_type=F32)

        further_windows(todo, run)

    tiles(lo, hi, tile)


def prepare_kernel(active_s, keys_any, keys_v, table_hbm, adj_out, local_out, counts, adj, acc, table, keys_s, sems):
    scalars = pltpu.make_async_copy(keys_any, keys_s, sems.at[3])
    scalars.start()
    load = pltpu.make_async_copy(table_hbm, table, sems.at[2])
    load.start()
    adj[...] = jnp.zeros_like(adj)
    scalars.wait()
    boundary = local_edges(keys_s)
    build_adjacency(keys_s, keys_v, adj, boundary, active_s[0] * 128)
    save_adj = pltpu.make_async_copy(adj.at[pl.ds(0, PART), :], adj_out, sems.at[0])
    save_adj.start()
    acc[...] = jnp.zeros_like(acc)
    load.wait()
    aggregate_local(keys_s, keys_v, table, acc, 0, boundary)
    save_acc = pltpu.make_async_copy(acc.at[pl.ds(0, PART), :], local_out, sems.at[1])
    save_acc.start()

    def tally(t, total):
        keys = [keys_v[32 * t + j] for j in range(32)]
        high = jnp.concatenate(
            [one_hot((iota((32, 128), 0) == (target_of(k) >> 7)) & (k < ACTIVE_END)) for k in keys], axis=1
        )
        low = jnp.concatenate([one_hot(iota((128, 128), 0) == (target_of(k) & 127)) for k in keys], axis=1)
        return total + lax.dot_general(high, low, (((1,), (1,)), ((), ())), preferred_element_type=F32)

    total = lax.fori_loop(0, EDGES // 4096, tally, jnp.zeros((32, 128), F32))
    upper = jnp.floor(total * (1.0 / 256.0))
    lower = total - upper * 256.0
    for s in range(4):
        both = jnp.concatenate([upper[8 * s : 8 * s + 8], lower[8 * s : 8 * s + 8]], axis=1)
        counts[s] = jnp.concatenate([both, jnp.zeros((8, WIDTH), F32)], axis=0).astype(BF16)
    save_adj.wait()
    save_acc.wait()


def transpose_kernel(adj, out):
    out[0] = jnp.transpose(adj[...])


def forward_remote_kernel(shifts, owner_s, table, counts, adj_hbm, local_hbm, *refs):
    outs, (adj, local_part, sems) = refs[:-3], refs[-3:]
    halves = ROWS // FINE
    loads = []
    for n in range(len(outs)):
        for h in range(halves):
            rows = pl.ds(pl.multiple_of(owner_s[shifts[n]] * ROWS + h * FINE, FINE), FINE)
            i = n * halves + h
            pair = (
                pltpu.make_async_copy(adj_hbm.at[rows, :], adj.at[i], sems.at[0, i]),
                pltpu.make_async_copy(local_hbm.at[rows, :], local_part.at[i], sems.at[1, i]),
            )
            for copy in pair:
                copy.start()
            loads.append(pair)
    for n, out in enumerate(outs):
        out[ROWS:, :] = counts[owner_s[shifts[n]]]
        for h in range(halves):
            i = n * halves + h
            for copy in loads[i]:
                copy.wait()
            total = local_part[i] + jnp.dot(adj[i], table[...], preferred_element_type=F32)
            out[h * FINE : h * FINE + FINE, :] = total.astype(BF16)


def pick_kernel(senders, table, out, acc):
    for c in range(8):
        col = key_column(senders[c : c + 1, :])
        pick = jnp.concatenate([one_hot(col == iota((128, 128), 1) + 128 * k) for k in range(ROWS // 128)], axis=1)
        acc[:, c, :] = jnp.dot(pick, table[...], preferred_element_type=F32)
    out[...] = acc[...].astype(BF16)


def combine_kernel(senders, returned, kept, out_hbm, out, sems):
    saves = []
    for i in range(4):
        rows = pl.ds(i * (ROWS // 4), ROWS // 4)
        nodes = iota((ROWS // 4, 128), 0) + i * (ROWS // 4)
        place = jnp.concatenate([one_hot(nodes == senders[j]) for j in range(ROWS // 128)], axis=1)
        out[rows, :] = kept[rows, :] + jnp.dot(place, returned[...], preferred_element_type=F32)
        saves.append(pltpu.make_async_copy(out.at[rows, :], out_hbm.at[rows, :], sems.at[i]))
        saves[i].start()
    for copy in saves:
        copy.wait()


def dense_kernel(feats, cots, w_self, w_neigh, bias, *refs):
    parts, counts, (acts, scaled, up_out, inv_ref) = refs[:4], refs[4:8], refs[8:]
    i = pl.program_id(0)

    @pl.when(i == 0)
    def _():
        deg = jnp.zeros((8, 128), F32)
        for s in range(4):
            c = counts[s][...].astype(F32)
            deg = deg + c[:8, :128] * 256.0 + c[:8, 128:]
        inv = 1.0 / jnp.maximum(deg, 1.0)
        for r in range(8):
            inv_ref[r] = inv[r : r + 1]

    cols = [key_column(inv_ref[4 * i + r]) for r in range(4)]
    inverse = jnp.concatenate([jnp.concatenate([c, c], axis=1) for c in cols], axis=0)
    totals = parts[0][...].astype(F32)
    for s in range(1, 4):
        totals = totals + parts[s][...].astype(F32)
    mean = (totals * inverse).astype(BF16)
    pre = (
        jnp.dot(feats[...], w_self[...], preferred_element_type=F32)
        + jnp.dot(mean, w_neigh[...], preferred_element_type=F32)
        + bias[...].astype(F32)
    )
    sigma = jax.nn.sigmoid(pre)
    acts[...] = (pre * sigma).astype(BF16)
    slope = sigma * (1.0 + pre * (1.0 - sigma))
    up = (cots[...].astype(F32) * slope).astype(BF16)
    back = lax.dot_general(up, w_neigh[...], (((1,), (1,)), ((), ())), preferred_element_type=F32)
    scaled[...] = (back * inverse).astype(BF16)
    up_out[...] = up


def scatter_back(keys_s, active_s, keys_v, spread, rows_ref, acc, remote):
    lo, hi = edge_range(keys_s, active_s, remote)

    def tile(t, carry):
        rows = [keys_v[4 * t + j] for j in range(4)]
        for sub in range(CHUNK // SUB):
            base, count = sub_range(keys_s, t * CHUNK + sub * SUB, lo, hi, BACK)
            cols = [target_of(key_column(rows[2 * sub + j])) for j in range(2)]

            def window(w):
                off = pl.multiple_of(base + w * BACK, 16)
                pick = jnp.concatenate(
                    [
                        jnp.concatenate(
                            [one_hot(c - off == iota((128, 128), 1) + 128 * k) for k in range(BACK // 128)], axis=1
                        )
                        for c in cols
                    ],
                    axis=0,
                )
                return jnp.dot(pick, spread[pl.ds(off, BACK), :], preferred_element_type=F32)

            rows_ref[sub * SUB : (sub + 1) * SUB, :] = window(0)

            def more(w, c):
                rows_ref[sub * SUB : (sub + 1) * SUB, :] += window(w)
                return c

            lax.fori_loop(1, count, more, 0)
        place = jnp.concatenate(
            [one_hot(iota((ROWS, 128), 0) == source_of(rows[j], remote)) for j in range(4)], axis=1
        )
        acc[...] += jnp.dot(place, rows_ref[...].astype(BF16), preferred_element_type=F32)
        return carry

    lax.fori_loop(lo // CHUNK, (hi + CHUNK - 1) // CHUNK, tile, 0)


def piece_sum(owner_s, pieces, adj, start):
    halves = ROWS // CHUNK
    total = start
    for shift, piece in pieces:
        for h in range(halves):
            rows = piece[h * CHUNK : h * CHUNK + CHUNK, :]
            part = jnp.dot(adj[owner_s[shift] * halves + h], rows, preferred_element_type=F32)
            total = part if total is None else total + part
    return total


def backward_first_kernel(owner_s, own, far, adj, out):
    out[...] = piece_sum(owner_s, ((0, own), (2, far)), adj, None)


def backward_last_kernel(owner_s, left, right, start, adj, out):
    out[...] = piece_sum(owner_s, ((3, left), (1, right)), adj, start[...]).astype(BF16)


def backward_local_kernel(keys_s, active_s, owner_s, keys_v, up, w_self, p0, p1, p2, p3, out, spread, rows_ref, sems):
    loads = []
    for n, (shift, piece) in enumerate(((0, p0), (3, p1), (1, p2), (2, p3))):
        rows = pl.ds(pl.multiple_of(owner_s[shift] * ROWS, ROWS), ROWS)
        loads.append(pltpu.make_async_copy(piece, spread.at[rows, :], sems.at[n]))
        loads[n].start()
    spread[PART:, :] = jnp.zeros((BACK, WIDTH), BF16)
    out[...] = lax.dot_general(up[...], w_self[...], (((1,), (1,)), ((), ())), preferred_element_type=F32)
    for copy in loads:
        copy.wait()
    scatter_back(keys_s, active_s, keys_v, spread, rows_ref, out, 0)


VMEM = pl.BlockSpec(memory_space=pltpu.VMEM)
ANY = pl.BlockSpec(memory_space=pl.ANY)
HBM = pl.BlockSpec(memory_space=pltpu.HBM)
def params(mib):
    return pltpu.CompilerParams(vmem_limit_bytes=mib << 20)


def local(features, cotangent, w_self, w_neigh, bias, send_rows, edge_src, edge_dst, tile_count):
    peers, capacity = send_rows.shape[2], send_rows.shape[3]
    shape = jax.ShapeDtypeStruct
    picked = pl.pallas_call(
        pick_kernel,
        grid=(1,),
        in_specs=[
            pl.BlockSpec((capacity, peers), lambda i: (0, 0)),
            pl.BlockSpec((ROWS, WIDTH), lambda i: (0, 0)),
        ],
        out_specs=pl.BlockSpec((peers, capacity, WIDTH), lambda i: (0, 0, 0)),
        out_shape=shape((peers, capacity, WIDTH), BF16),
        scratch_shapes=[pltpu.VMEM((peers, capacity, WIDTH), F32)],
        compiler_params=params(8),
        name="pick_rows",
    )(in_hbm(jnp.transpose(send_rows.reshape(peers, capacity))), in_hbm(features))
    remote = lax.all_to_all(picked, "dom", split_axis=0, concat_axis=0, tiled=True).reshape(peers * capacity, WIDTH)

    sources = edge_src.reshape(EDGES)
    targets = edge_dst.reshape(EDGES)
    active = tile_count.reshape(1)
    live = jnp.arange(EDGES, dtype=jnp.int32) < active[0] * 128
    keys = ((sources >> 10) << 22) + (targets << 10) + (sources & 1023)
    keys_s = lax.sort(jnp.where(live, keys, ACTIVE_END))
    keys_v = keys_s.reshape(EDGES // 128, 1, 128)

    adj, before, counts = pl.pallas_call(
        prepare_kernel,
        grid_spec=pltpu.PrefetchScalarGridSpec(
            num_scalar_prefetch=1,
            grid=(),
            in_specs=[ANY, VMEM, HBM],
            out_specs=(HBM, HBM, VMEM),
            scratch_shapes=[
                pltpu.VMEM((PADDED, ROWS), BF16),
                pltpu.VMEM((PADDED, WIDTH), F32),
                pltpu.VMEM((ROWS, WIDTH), BF16),
                pltpu.SMEM((EDGES,), jnp.int32),
                pltpu.SemaphoreType.DMA((4,)),
            ],
        ),
        out_shape=(
            pltpu.HBM((PART, ROWS), BF16),
            pltpu.HBM((PART, WIDTH), F32),
            shape((4, CNT, WIDTH), BF16),
        ),
        compiler_params=params(30),
        name="prepare",
    )(active, keys_s, keys_v, in_hbm(features))
    chunks = PART // CHUNK
    rank = lax.axis_index("src")

    order = lax.optimization_barrier((rank + jnp.arange(4, dtype=jnp.int32)) % 4)

    def shifted(x, k):
        return lax.ppermute(x, "src", [(j, (j + k) % 4) for j in range(4)])

    def partials(table, *shifts):
        count = len(shifts)
        return pl.pallas_call(
            functools.partial(forward_remote_kernel, shifts),
            grid_spec=pltpu.PrefetchScalarGridSpec(
                num_scalar_prefetch=1,
                grid=(),
                in_specs=[VMEM, VMEM, HBM, HBM],
                out_specs=[VMEM] * count,
                scratch_shapes=[
                    pltpu.VMEM((ROWS // FINE * count, FINE, ROWS), BF16),
                    pltpu.VMEM((ROWS // FINE * count, FINE, WIDTH), F32),
                    pltpu.SemaphoreType.DMA((2, ROWS // FINE * count)),
                ],
            ),
            out_shape=[shape((ROWS + CNT, WIDTH), BF16)] * count,
            compiler_params=params(12),
            name="aggregate_remote_" + "_".join(str(k) for k in shifts),
        )(order, table, counts, in_hbm(adj), in_hbm(before))

    (partial_far,) = partials(remote, 2)
    from_far = shifted(partial_far, 2)
    remote, partial_far = lax.optimization_barrier((remote, partial_far))
    partial_next, partial_prev = partials(remote, 1, 3)
    from_prev = shifted(partial_next, 1)
    from_next = shifted(partial_prev, 3)
    remote, partial = lax.optimization_barrier((remote, partial_next))
    (partial_own,) = partials(remote, 0)
    adj, partial = lax.optimization_barrier((adj, partial))
    adj_t = pl.pallas_call(
        transpose_kernel,
        grid=(chunks,),
        in_specs=[pl.BlockSpec((CHUNK, ROWS), lambda i: (i, 0))],
        out_specs=pl.BlockSpec((1, ROWS, CHUNK), lambda i: (i, 0, 0)),
        out_shape=shape((chunks, ROWS, CHUNK), BF16),
        compiler_params=params(10),
        name="adjacency_transposed",
    )(in_hbm(adj))
    adj_t, from_far = lax.optimization_barrier((adj_t, from_far))

    block = ROWS // 2
    tile = pl.BlockSpec((block, WIDTH), lambda i: (i, 0))
    whole = pl.BlockSpec((WIDTH, WIDTH), lambda i: (0, 0))
    count_rows = pl.BlockSpec((CNT, WIDTH), lambda i: (ROWS // CNT, 0))
    received = (partial_own, from_prev, from_next, from_far)
    acts, scaled, up = pl.pallas_call(
        dense_kernel,
        grid=(2,),
        in_specs=[tile, tile, whole, whole, pl.BlockSpec((1, WIDTH), lambda i: (0, 0))]
        + [tile] * 4
        + [count_rows] * 4,
        out_specs=(tile, tile, tile),
        out_shape=(shape((ROWS, WIDTH), BF16), pltpu.HBM((ROWS, WIDTH), BF16), pltpu.HBM((ROWS, WIDTH), BF16)),
        scratch_shapes=[pltpu.VMEM((8, 1, 128), F32)],
        compiler_params=params(14),
        name="dense_layer",
    )(features, in_hbm(cotangent), w_self, w_neigh, bias.reshape(1, WIDTH), *received, *received)
    far = shifted(scaled, 2)
    prev = shifted(scaled, 1)
    follow = shifted(scaled, 3)

    def backward(kernel, pieces, dtype, name):
        return pl.pallas_call(
            kernel,
            grid_spec=pltpu.PrefetchScalarGridSpec(
                num_scalar_prefetch=1, grid=(), in_specs=[VMEM] * (len(pieces) + 1), out_specs=VMEM
            ),
            out_shape=shape((ROWS, WIDTH), dtype),
            compiler_params=params(8),
            name=name,
        )(order, *pieces, adj_t)

    begun = backward(backward_first_kernel, (scaled, far), F32, "scatter_first")
    outgoing = backward(backward_last_kernel, (prev, follow, begun), BF16, "scatter_last")
    returned = lax.all_to_all(
        outgoing.reshape(peers, capacity, WIDTH), "dom", split_axis=0, concat_axis=0, tiled=True
    ).reshape(peers * capacity, WIDTH)
    kept = pl.pallas_call(
        backward_local_kernel,
        grid_spec=pltpu.PrefetchScalarGridSpec(
            num_scalar_prefetch=3,
            grid=(),
            in_specs=[VMEM] * 3 + [ANY] * 4,
            out_specs=VMEM,
            scratch_shapes=[
                pltpu.VMEM((PADDED, WIDTH), BF16),
                pltpu.VMEM((CHUNK, WIDTH), F32),
                pltpu.SemaphoreType.DMA((4,)),
            ],
        ),
        out_shape=shape((ROWS, WIDTH), F32),
        compiler_params=params(10),
        name="scatter_local",
    )(keys_s, active, order, keys_v, up, w_self, scaled, prev, follow, far)
    total = pl.pallas_call(
        combine_kernel,
        in_specs=[VMEM] * 3,
        out_specs=HBM,
        out_shape=pltpu.HBM((ROWS, WIDTH), F32),
        scratch_shapes=[pltpu.VMEM((ROWS, WIDTH), F32), pltpu.SemaphoreType.DMA((4,))],
        compiler_params=params(8),
        name="combine",
    )(send_rows.reshape(peers * capacity // 128, 1, 128), returned, kept)
    return acts, total


def solution(mesh):
    placed = (
        P(("dom", "src"), None),
        P(("dom", "src"), None),
        P(),
        P(),
        P(),
        P("dom", "src", None, None),
        P("dom", "src", None),
        P("dom", "src", None),
        P("dom", "src"),
    )
    return jax.shard_map(
        local,
        mesh=mesh,
        in_specs=placed,
        out_specs=(P(("dom", "src"), None), P(("dom", "src"), None)),
        check_vma=False,
    )
```
